256 devices in a mesh: rec: 8 (over y, core), tm: 32 (over x, z).
Axes of the slice: x: 4, y: 4, z: 8, core: 2. Of those that a mesh axis runs over, the one named last changes fastest.
Arguments:
- frames: bfloat16 [8, 16384, 1024], P('rec', 'tm'), may hold values from -6 to 6
- lengths: int32 [8], P('rec'), may hold values from 4096 to 16384, as said below
- norm_gain: float32 [1024], replicated, may hold values from 0.1 to 1.9
- memory_gain: float32 [1024], replicated, may hold values from 0.1 to 1.9
- qkv_weight: bfloat16 [3, 1024, 1024], P(None, None, 'tm'), may hold values from -3.75 to 3.75
- out_weight: bfloat16 [1024, 1024], P(None, 'tm'), may hold values from -0.1875 to 0.1875
- segment_ids: int32 [8, 32, 512], P('rec', 'tm'), may hold values from 0 to 127, never falling along the last dimension, each value on 1 to 12 neighbouring positions
- owners: int32 [8, 32, 128, 1], P('rec', 'tm'), may hold values from 0 to 31; in each aligned block of 128 rows (0 to 127, 128 to 255, ..., all dimensions but the last counted through in order) at most 8 rows name the same one
- language_weight: bfloat16 [1024, 2048], P(None, 'rec'), may hold values from -0.1875 to 0.1875
Outputs:
- encoded: bfloat16 [8, 16384, 1024], P('rec', 'tm')
- lm_rows: bfloat16 [8, 32, 256, 2048], P('rec', 'tm')
The draws below stay inside these ranges and needn't reach their ends.
Inputs may be any that keep to these rules, and one draw needn't show every extreme that they name: `lengths`: one recording has exactly 16384 live frames. `segment_ids`: in each block, token numbers never fall and each of the 128 tokens has 1 to 12 frames, one exactly 12. `owners`: within the 128 tokens of one block no owner is named more than 8 times, a bound that some block reaches.
All inputs are finite; a program needn't handle non-finite values.
Results may differ from the reference program's by a relative error of at most 0.035.
Values may be sent and summed in bfloat16 or wider, within the bound.
A program may use at most 64 MiB of HBM per device.

```python
import math
import jax
import jax.numpy as jnp
import numpy as np
from jax import lax

D = 1024
H = 16
DL = 2048
C = 32
RC = 8
SEG_MOST = 12
F_DEV = 512
TOK_DEV = 128
CAP = 8
SLOTS = 256
REC = 8
FRAMES = 16384
N_TM = 32


def draw_lengths(key, part):
    first_key, second_key = jax.random.split(key)
    drawn = jax.random.randint(first_key, (REC,), FRAMES // 4, FRAMES + 1)
    picked = jax.random.randint(second_key, (), 0, REC)
    return jnp.where(jnp.arange(REC) == picked, FRAMES, drawn).astype(jnp.int32)


def draw_qkv_weight(key, part):
    base_draw = jax.random.normal(key, (3, D, D), jnp.float32)
    base_draw = jnp.clip(base_draw, -6.0, 6.0) * D ** (-0.5)
    base_draw = jnp.clip(base_draw, -3.75, 3.75)
    return base_draw.astype(jnp.bfloat16)


def steps_of(own_key, shape, cuts, low, largest):
    loudness = 1.0
    for axis_at, parts in cuts:
        steps = jax.random.uniform(jax.random.fold_in(jax.random.fold_in(own_key, 6), axis_at), (parts,), jnp.float32, low / len(cuts), largest / len(cuts))
        loudness = loudness * jnp.repeat(jnp.exp(steps), shape[axis_at] // parts).reshape((-1,) + (1,) * (len(shape) - 1 - axis_at))
    return loudness


def length_profile(count, total, bound, lean):
    portions = [(1 << 20) // math.isqrt(grade ** lean) + 1 for grade in range(2, count + 1)]
    surplus, given = total - bound - (count - 1), [1] * (count - 1)
    while surplus > 0:
        free = [i for i in range(count - 1) if given[i] < bound]
        pool, left = sum([portions[i] for i in free]), surplus
        for i in free:
            extra = min(bound - given[i], max(1, left * portions[i] // pool), surplus)
            given[i] = given[i] + extra
            surplus = surplus - extra
    return np.array([bound] + given)


def uneven_parts(key, amount, total, bound, skew):
    if amount == 2:
        one = jax.random.randint(key, (), max(1, total - bound), min(bound, total - 1) + 1)
        return jnp.stack([one, total - one])
    sizes = jnp.asarray(length_profile(amount, total, bound, skew), jnp.int32)
    couples = (amount - 1) // 2
    donor, sink = sizes[1:1 + 2 * couples:2], sizes[2:2 + 2 * couples:2]
    room = jnp.minimum(donor - 1, bound - sink)
    moved = jax.random.randint(jax.random.fold_in(key, 1), (couples,), 0, 1 << 20) % (room + 1)
    sizes = sizes.at[1:1 + 2 * couples:2].set(donor - moved).at[2:2 + 2 * couples:2].set(sink + moved)
    return sizes[jax.random.permutation(jax.random.fold_in(key, 2), amount)]


def routed_block(rng, own, number, rows, number_of, top, most, slope):
    order = jax.random.permutation(rng, number_of)
    heavy_load, ordinary = load_shares(number_of, rows * top, most, slope, True), load_shares(number_of, rows * top, most, slope, False)
    places = jnp.arange(number_of)

    def named(sizes, offset_by):
        used = int((sizes > 0).sum())
        fixed = max(1, used // 4)
        shifted = fixed + (places - fixed + offset_by * (used - fixed)) % max(1, number_of - fixed)
        return jnp.zeros((number_of,), jnp.int32).at[order[jnp.where(places < fixed, places, shifted)]].set(jnp.asarray(sizes, jnp.int32))

    sizes = jnp.where(number % 4 == 0, named(heavy_load, number // 4), named(ordinary, number - number // 4 - 1))
    mixed = jax.random.permutation(jax.random.fold_in(own, 3), number_of)
    giver, taker = mixed[0:number_of // 2 * 2:2], mixed[1:number_of // 2 * 2:2]
    room = jnp.minimum(sizes[giver] - 1, most - sizes[taker]) // 2
    room = jnp.where((giver == order[0]) | (taker == order[0]) | (sizes[taker] == 0), 0, jnp.maximum(room, 0))
    shifted = jax.random.randint(jax.random.fold_in(own, 4), (number_of // 2,), 0, 1 << 20) % (room + 1)
    sizes = sizes.at[giver].add(-shifted).at[taker].add(shifted)
    labels = jnp.searchsorted(jnp.cumsum(sizes), jnp.arange(rows * top), side="right").astype(jnp.int32)
    grid = labels.reshape(top, rows).T
    grid = grid[jax.random.permutation(jax.random.fold_in(own, 1), rows)]
    offset_by = jax.random.randint(jax.random.fold_in(own, 2), (rows, 1), 0, top)
    return jnp.take_along_axis(grid, (jnp.arange(top)[None, :] + offset_by) % top, axis=1)


def load_shares(count, total, reach, slope, full):
    portions = [(1 << 20) // math.isqrt(standing ** slope) + 1 for standing in range(1, count + 1)]
    largest = reach if full else min(reach, max(-(-total // count), total * portions[0] // sum(portions)))
    least = 1 if total - largest >= count - 1 else 0
    holding, surplus = [largest] + [least] * (count - 1), total - largest - least * (count - 1)
    while surplus > 0:
        movable = [i for i in range(1, count) if holding[i] < largest] or [i for i in range(1, count) if holding[i] < reach]
        mass, budget = sum([portions[i] for i in movable]), surplus
        for i in movable:
            extra = min(reach - holding[i], max(1, budget * portions[i] // mass), surplus)
            holding[i] = holding[i] + extra
            surplus = surplus - extra
    return np.array(holding)


def scatter_about(stream_key, extent, width, most, pieces=(), held_as=jnp.bfloat16):
    factor_of = steps_of(stream_key, extent, pieces, -0.22, 0.18) if pieces else 1.0
    values = jax.random.normal(stream_key, extent, jnp.float32) * width * factor_of
    return jnp.minimum(jnp.maximum(values, -most), most).astype(held_as)


def setup_inputs(seed: int = 0) -> dict:
    splits = jax.random.split(jax.random.key(seed), 10)
    frames = scatter_about(splits[0], (REC, FRAMES, D), 1.0, 6.0, ((0, 8), (1, 32)))
    lengths = draw_lengths(jax.random.fold_in(splits[9], 71), 0)
    norm_gain = jnp.clip(1.0 + 0.18 * jax.random.normal(splits[2], (D,), jnp.float32), 0.1, 1.9)
    memory_gain = jnp.clip(1.0 + 0.18 * jax.random.normal(splits[3], (D,), jnp.float32), 0.1, 1.9)
    qkv_weight = draw_qkv_weight(jax.random.fold_in(splits[9], 71), 0)
    out_weight = scatter_about(splits[5], (D, D), D ** -0.5, 0.1875, ((1, 32),))
    segment_ids = jax.vmap(lambda own: jnp.searchsorted(jnp.cumsum(uneven_parts(own, TOK_DEV, F_DEV, SEG_MOST, 2)), jnp.arange(F_DEV), side="right"))(jax.random.split(splits[6], REC * N_TM)).reshape((REC, N_TM, F_DEV)).astype(jnp.int32)
    owners_keys = jax.random.split(jax.random.fold_in(splits[7], 1), REC * N_TM * TOK_DEV // TOK_DEV)
    owners_turns = jax.random.permutation(jax.random.fold_in(splits[7], 3), REC * N_TM * TOK_DEV // TOK_DEV)
    owners = jax.vmap(lambda own, number: routed_block(jax.random.fold_in(splits[7], 2), own, number, TOK_DEV, N_TM, 1, CAP, 2))(owners_keys, owners_turns).reshape((REC, N_TM, TOK_DEV, 1))
    language_weight = scatter_about(splits[8], (D, DL), D ** -0.5, 0.1875, ((1, 8),))
    return dict(frames=frames, lengths=lengths, norm_gain=norm_gain, memory_gain=memory_gain, qkv_weight=qkv_weight, out_weight=out_weight, segment_ids=segment_ids, owners=owners, language_weight=language_weight)


EPS_NORM = 1e-05
EPS_MEMORY = 1e-06
NEG_BIG = -1e+30

def layer_norm(values_in, gain):
    values_in = values_in.astype(jnp.float32)
    centre = lax.optimization_barrier(jnp.mean(values_in, axis=-1, keepdims=True))
    centred = values_in - centre
    spread = lax.optimization_barrier(jnp.mean(centred * centred, axis=-1, keepdims=True))
    return centred * lax.rsqrt(spread + EPS_NORM) * gain

def span_memory(normed, live_mask, gain, span_len):
    model_width = normed.shape[1]
    masked = jnp.where(live_mask[:, None], normed.astype(jnp.float32), jnp.float32(0.0))
    owner_sums = masked.reshape(-1, span_len, model_width).sum(axis=1)
    counts = live_mask.reshape(-1, span_len).astype(jnp.float32).sum(axis=1)
    means = owner_sums / jnp.maximum(counts, 1.0)[:, None]
    power = lax.optimization_barrier(jnp.mean(means * means, axis=-1, keepdims=True))
    return (means * lax.rsqrt(power + EPS_MEMORY) * gain).astype(jnp.bfloat16)

def block_size(frame_count):
    return 256 if frame_count % 256 == 0 else 128

def local_part(query, keys, values, first_frame, length, head_count, span_len, right_len):
    frame_count, model_width = query.shape
    head_size = model_width // head_count
    group_rows = 4 * span_len
    group_count = frame_count // group_rows
    block_rows = block_size(frame_count)
    query_blocks = query.reshape(group_count, group_rows, head_count, head_size).astype(jnp.float32)
    key_blocks = keys[:frame_count].reshape(group_count, group_rows, head_count, head_size)
    value_blocks = values[:frame_count].reshape(group_count, group_rows, head_count, head_size)
    key_tail = keys[frame_count:].reshape(1, right_len, head_count, head_size)
    value_tail = values[frame_count:].reshape(1, right_len, head_count, head_size)
    key_all = jnp.concatenate([key_blocks, jnp.concatenate([key_blocks[1:, :right_len], key_tail], axis=0)], axis=1)
    value_all = jnp.concatenate([value_blocks, jnp.concatenate([value_blocks[1:, :right_len], value_tail], axis=0)], axis=1)
    start_offsets = jnp.arange(group_count, dtype=jnp.int32)[:, None] * group_rows
    query_pos = first_frame + start_offsets + jnp.arange(group_rows, dtype=jnp.int32)[None, :]
    key_pos = first_frame + jnp.concatenate([start_offsets + jnp.arange(group_rows, dtype=jnp.int32)[None, :], start_offsets + group_rows + jnp.arange(right_len, dtype=jnp.int32)[None, :]], axis=1)
    query_span = query_pos // span_len
    span_end = (query_span + 1) * span_len
    same = (key_pos // span_len)[:, None, :] == query_span[:, :, None]
    ahead = (key_pos[:, None, :] >= span_end[:, :, None]) & (key_pos[:, None, :] < span_end[:, :, None] + right_len)
    allowed = (same | ahead) & (key_pos < length)[:, None, :]
    scores = jnp.einsum('gqhd,gkhd->ghqk', query_blocks, key_all.astype(jnp.float32)) * head_size ** (-0.5)
    scores = jnp.where(allowed[:, None], scores, NEG_BIG)
    row_peak = lax.optimization_barrier(jnp.max(scores, axis=-1))
    weights = jnp.where(allowed[:, None], jnp.exp(scores - row_peak[..., None]), jnp.float32(0.0))
    row_total = lax.optimization_barrier(jnp.sum(weights, axis=-1))
    accum = jnp.einsum('ghqk,gkhd->ghqd', weights.astype(jnp.bfloat16).astype(jnp.float32), value_all.astype(jnp.float32))
    block_count = frame_count // block_rows
    row_peak = row_peak.transpose(1, 0, 2).reshape(head_count, block_count, block_rows).transpose(1, 0, 2)
    row_total = row_total.transpose(1, 0, 2).reshape(head_count, block_count, block_rows).transpose(1, 0, 2)
    accum = accum.transpose(1, 0, 2, 3).reshape(head_count, block_count, block_rows, head_size).transpose(1, 0, 2, 3)
    return (row_peak, row_total, accum)

def memory_update(carry, memory_keys, memory_values, start, query, first_frame, length, head_count, span_len):
    row_peak, row_total, accum = carry
    block_count, _, block_rows = row_peak.shape
    row_count, model_width = memory_keys.shape
    head_size = model_width // head_count
    mem_keys = memory_keys.reshape(row_count, head_count, head_size).astype(jnp.float32)
    mem_values = memory_values.reshape(row_count, head_count, head_size).astype(jnp.float32)
    mem_index = start + jnp.arange(row_count, dtype=jnp.int32)
    mem_live = mem_index * span_len < length
    query_blocks = query.reshape(block_count, block_rows, head_count, head_size)
    positions = first_frame + jnp.arange(block_count * block_rows, dtype=jnp.int32).reshape(block_count, block_rows)

    def one_block(packed):
        query_now, pos_now, peak_now, total_now, accum_now = packed
        scores = jnp.einsum('qhd,khd->hqk', query_now.astype(jnp.float32), mem_keys) * head_size ** (-0.5)
        allowed = (mem_index[None, :] < (pos_now // span_len)[:, None]) & mem_live[None, :]
        scores = jnp.where(allowed[None], scores, NEG_BIG)
        new_peak = jnp.maximum(peak_now, lax.optimization_barrier(jnp.max(scores, axis=-1)))
        weights = jnp.where(allowed[None], jnp.exp(scores - new_peak[..., None]), jnp.float32(0.0))
        factor = jnp.exp(peak_now - new_peak)
        total_next = total_now * factor + lax.optimization_barrier(jnp.sum(weights, axis=-1))
        accum_next = accum_now * factor[..., None] + jnp.einsum('hqk,khd->hqd', weights.astype(jnp.bfloat16).astype(jnp.float32), mem_values)
        return (new_peak, total_next, accum_next)
    return lax.map(one_block, (query_blocks, positions, row_peak, row_total, accum))

def finish(carry, frame_count, model_width):
    row_peak, row_total, accum = carry
    result = accum / row_total[..., None]
    return result.transpose(0, 2, 1, 3).reshape(frame_count, model_width).astype(jnp.bfloat16)

def dispatch_matrix(owner_ids, owner_count, capacity):
    choose = (owner_ids[:, None] == jnp.arange(owner_count, dtype=jnp.int32)[None, :]).astype(jnp.int32)
    before = jnp.cumsum(choose, axis=0) - choose
    slot_index = lax.optimization_barrier(jnp.sum(before * choose, axis=1))
    target = owner_ids * capacity + slot_index
    slot_rows = jnp.arange(owner_count * capacity, dtype=jnp.int32)
    return (slot_rows[:, None] == target[None, :]).astype(jnp.bfloat16)

def reference(frames, lengths, norm_gain, memory_gain, qkv_weight, out_weight, segment_ids, owners, language_weight):

    def one_recording(packed):
        rec_frames, length, rec_segments, rec_owners = packed
        normed = layer_norm(rec_frames, norm_gain).astype(jnp.bfloat16)
        live_mask = jnp.arange(FRAMES, dtype=jnp.int32) < length
        memory = span_memory(normed, live_mask, memory_gain, C)
        query = jnp.dot(normed, qkv_weight[0], preferred_element_type=jnp.float32).astype(jnp.bfloat16)
        keys = jnp.dot(normed, qkv_weight[1], preferred_element_type=jnp.float32).astype(jnp.bfloat16)
        values = jnp.dot(normed, qkv_weight[2], preferred_element_type=jnp.float32).astype(jnp.bfloat16)
        memory_keys = jnp.dot(memory, qkv_weight[1], preferred_element_type=jnp.float32).astype(jnp.bfloat16)
        memory_values = jnp.dot(memory, qkv_weight[2], preferred_element_type=jnp.float32).astype(jnp.bfloat16)
        padding = jnp.zeros((RC, D), jnp.bfloat16)
        keys_padded = jnp.concatenate([keys, padding], axis=0)
        values_padded = jnp.concatenate([values, padding], axis=0)

        def one_block(block_id):
            first_frame = (block_id * F_DEV).astype(jnp.int32)
            query_now = lax.dynamic_slice_in_dim(query, first_frame, F_DEV, 0)
            keys_now = lax.dynamic_slice_in_dim(keys_padded, first_frame, F_DEV + RC, 0)
            values_now = lax.dynamic_slice_in_dim(values_padded, first_frame, F_DEV + RC, 0)
            carry = local_part(query_now, keys_now, values_now, first_frame, length, H, C, RC)
            carry = memory_update(carry, memory_keys, memory_values, 0, query_now, first_frame, length, H, C)
            return finish(carry, F_DEV, D)
        attended = lax.map(one_block, jnp.arange(N_TM, dtype=jnp.int32)).reshape(FRAMES, D)
        projected = jnp.dot(attended, out_weight, preferred_element_type=jnp.float32)
        encoded = jnp.where(live_mask[:, None], rec_frames.astype(jnp.float32) + projected, jnp.float32(0.0)).astype(jnp.bfloat16)
        encoder_blocks = encoded.reshape(N_TM, F_DEV, D)
        owner_indicator = (rec_segments[:, None, :] == jnp.arange(TOK_DEV, dtype=jnp.int32)[None, :, None]).astype(jnp.float32)
        owner_sums = jnp.einsum('xqe,xem->xqm', owner_indicator, encoder_blocks.astype(jnp.float32))
        counts = lax.optimization_barrier(jnp.sum(owner_indicator, axis=-1))
        pooled_rows = (owner_sums / counts[..., None]).astype(jnp.bfloat16)
        route_matrix = jax.vmap(lambda owner_ids: dispatch_matrix(owner_ids, N_TM, CAP))(rec_owners[:, :, 0])
        sent_rows = jnp.einsum('hag,hgw->haw', route_matrix.astype(jnp.float32), pooled_rows.astype(jnp.float32)).astype(jnp.bfloat16)
        received = sent_rows.reshape(N_TM, N_TM, CAP, D).transpose(1, 0, 2, 3).reshape(N_TM * SLOTS, D)
        lm_out = jnp.dot(received, language_weight, preferred_element_type=jnp.float32).astype(jnp.bfloat16)
        return (encoded, lm_out.reshape(N_TM, SLOTS, DL))
    encoded, lm_rows = lax.map(one_recording, (frames, lengths, segment_ids, owners))
    return (encoded, lm_rows)
```

```python
import functools

import jax
import jax.numpy as jnp
from jax import lax
from jax.experimental import pallas as pl
from jax.experimental.pallas import tpu as pltpu
from jax.sharding import PartitionSpec as P

H = 16
C = 32
RC = 8
EPS_NORM = 1e-05
EPS_MEMORY = 1e-06
NEG_BIG = -1e30

NX, NZ, NY = 4, 8, 4
N_TM = NX * NZ
F = 512
D = 1024
DL = 2048
TOK = 128
CAP = 8
SLOTS = 256
G = 4
GW = D // G
QB = 128
MEM = N_TM * F // C
KW = MEM + 2 * QB
BF = jnp.bfloat16
F32 = jnp.float32


def dot_nt(a, b):
    return lax.dot_general(a, b, (((1,), (1,)), ((), ())), preferred_element_type=F32)


def dot_nn(a, b):
    return lax.dot_general(a, b, (((1,), (0,)), ((), ())), preferred_element_type=F32)


def wrap(a, n):
    return lax.rem(a + 2 * n, n)


def kernel(
    frames, lengths, norm_gain, memory_gain, wq_hbm, wo_hbm, segments, owners, lw_hbm,
    enc_hbm, lm_hbm,
    wg, owg, lwg, xs, mg, mrows, q4, kk, vv, att, bias, ri, cnt, enc, sb, rb, lmo,
    w_send, w_recv, m_send, m_recv, o_send, o_recv, ws_send, ws_recv, os_send, os_recv,
    r_send, r_recv, l_send, l_recv, ls_send, ls_recv, a_send, a_recv, own_sem, out_sem,
):
    r = lax.axis_index("rec")
    t = lax.axis_index("tm")
    y, c = r // 2, lax.rem(r, 2)
    x, z = t // NZ, lax.rem(t, NZ)
    sib = (y * 2 + (1 - c), t)
    first_frame = t * F
    length = lengths[0]

    barrier = pltpu.get_barrier_semaphore()

    @pl.loop(1, N_TM)
    def _(d):
        pl.semaphore_signal(
            barrier, inc=1, device_id=(r, lax.rem(t + d, N_TM)), device_id_type=pl.DeviceIdType.MESH
        )

    @pl.loop(1, 2 * NY)
    def _(d):
        pl.semaphore_signal(
            barrier, inc=1, device_id=(lax.rem(r + d, 2 * NY), t), device_id_type=pl.DeviceIdType.MESH
        )

    pl.semaphore_wait(barrier, N_TM - 1 + 2 * NY - 1)

    def remote(src, dst, send, recv, device):
        return pltpu.make_async_remote_copy(
            src_ref=src,
            dst_ref=dst,
            send_sem=send,
            recv_sem=recv,
            device_id=device,
            device_id_type=pl.DeviceIdType.MESH,
        )

    steps = {
        0: [("z", k) for k in range(1, NZ // 2 + 1)] + [("x", k) for k in range(1, NX // 2 + 1)],
        1: [("x", k) for k in range(1, NX // 2 + 1)] + [("z", k) for k in range(1, NZ // 2 + 1)],
    }
    n_steps = len(steps[0])

    def size_pos(axis):
        return (NZ, z) if axis == "z" else (NX, x)

    def neighbour(axis, by):
        if axis == "z":
            return (r, x * NZ + wrap(z + by, NZ))
        return (r, wrap(x + by, NX) * NZ + z)

    def w_piece(v, axis, o):
        if v == 0:
            return wg.at[:, x, o, 0] if axis == "z" else wg.at[:, o, :, 0]
        return wg.at[:, o, z, 1] if axis == "x" else wg.at[:, :, o, 1]

    def o_piece(v, axis, o):
        if v == 0:
            return owg.at[x, o, 0] if axis == "z" else owg.at[o, :, 0]
        return owg.at[o, z, 1] if axis == "x" else owg.at[:, o, 1]

    def m_piece(v, axis, o):
        if v == 0:
            return mg.at[x, o] if axis == "z" else mg.at[o]
        return mg.at[o, z] if axis == "x" else mg.at[:, o]

    def cut(ref, axis, k, d):
        n = NZ if axis == "z" else NX
        if k < n // 2:
            return ref
        where = (slice(None),) * (len(ref.shape) - 1)
        return ref.at[where + (pl.ds(d * (D // 2), D // 2),)]

    def ring_start(v, i, piece, send, recv, own=None):
        axis, k = steps[v][i]
        n, pos = size_pos(axis)
        for d, s in enumerate((1, -1)):
            dst = cut(piece(v, axis, wrap(pos - s * (k - 1), n)), axis, k, d)
            src = own if own is not None and i == 0 else dst
            remote(src, dst, send.at[2 * i + d], recv.at[2 * i + d], neighbour(axis, s)).start()

    def ring_in(v, i, piece):
        axis, k = steps[v][i]
        n, pos = size_pos(axis)
        return [cut(piece(v, axis, wrap(pos - s * k, n)), axis, k, d) for d, s in enumerate((1, -1))]

    def ring_wait(v, i, piece, send, recv):
        axis, _ = steps[v][i]
        for d, ref in enumerate(ring_in(v, i, piece)):
            copy = remote(ref, ref, send.at[2 * i + d], recv.at[2 * i + d], neighbour(axis, 1))
            copy.wait_recv()
            copy.wait_send()

    def sib_start(v, i, piece, send, recv):
        for d, ref in enumerate(ring_in(v, i, piece)):
            remote(ref, ref, send.at[2 * i + d], recv.at[2 * i + d], sib).start()

    def sib_wait(v, i, piece, send, recv):
        for d, ref in enumerate(ring_in(v, i, piece)):
            remote(ref, ref, send.at[2 * i + d], recv.at[2 * i + d], sib).wait_send()
        for d, ref in enumerate(ring_in(1 - v, i, piece)):
            remote(ref, ref, send.at[2 * i + d], recv.at[2 * i + d], sib).wait_recv()

    def per_core(fn):
        for v in (0, 1):
            pl.when(c == v)(functools.partial(fn, v))

    own_copies = []
    for v in (0, 1):
        own_copies.append(
            pltpu.make_async_copy(wq_hbm.at[:, pl.ds(16 * v, 16)], wg.at[:, x, z, v], own_sem.at[v])
        )
        own_copies.append(
            pltpu.make_async_copy(wo_hbm.at[pl.ds(16 * v, 16)], owg.at[x, z, v], own_sem.at[2 + v])
        )
    own_copies.append(pltpu.make_async_copy(lw_hbm, lwg.at[r], own_sem.at[4]))

    def first_hop(v):
        ring_start(v, 0, w_piece, w_send, w_recv, own=wq_hbm.at[:, pl.ds(16 * v, 16)])

    per_core(first_hop)
    for copy in own_copies:
        copy.start()

    gain = norm_gain[...]

    @pl.loop(0, F // C)
    def _(i):
        rows = pl.ds(pl.multiple_of(i * C, C), C)
        v = frames[rows, :].astype(F32)
        centred = v - jnp.mean(v, axis=1, keepdims=True)
        spread = jnp.mean(centred * centred, axis=1, keepdims=True)
        normed = (centred * lax.rsqrt(spread + EPS_NORM) * gain).astype(BF)
        xs[rows, :] = normed
        start = first_frame + i * C
        live = start + lax.broadcasted_iota(jnp.int32, (C, 1), 0) < length
        total = jnp.sum(jnp.where(live, normed.astype(F32), 0.0), axis=0, keepdims=True)
        count = jnp.clip(length - start, 1, C).astype(F32)
        mrows[pl.ds(i, 1), :] = total / count

    means = mrows[...]
    power = jnp.mean(means * means, axis=1, keepdims=True)
    mg[x, z] = (means * lax.rsqrt(power + EPS_MEMORY) * memory_gain[...]).astype(BF)

    right = remote(
        xs.at[pl.ds(0, 16)], xs.at[pl.ds(F, 16)], r_send.at[0], r_recv.at[0], (r, wrap(t - 1, N_TM))
    )
    right.start()
    for copy in own_copies:
        copy.wait()

    def memory_hop(v):
        ring_start(v, 0, m_piece, m_send, m_recv)

    per_core(memory_hop)

    lw_up, lw_down = wrap(y + 1, NY), wrap(y - 1, NY)
    lw_far = wrap(y + 2, NY)

    def lw_half(slot, d):
        return lwg.at[slot, pl.ds(d * (D // 2), D // 2)]

    lw_first = [
        remote(lwg.at[r], lwg.at[r], l_send.at[0], l_recv.at[0], (lw_up * 2 + c, t)),
        remote(lwg.at[r], lwg.at[r], l_send.at[1], l_recv.at[1], (lw_down * 2 + c, t)),
        remote(lwg.at[r], lwg.at[r], ls_send.at[0], ls_recv.at[0], sib),
    ]

    span0 = t * (F // C)

    @pl.loop(0, F // QB)
    def _(b):
        q = b * QB + lax.broadcasted_iota(jnp.int32, (QB, KW), 0)
        n = lax.broadcasted_iota(jnp.int32, (QB, KW), 1)
        q_span = q // C
        u = b * QB + n - MEM
        in_memory = (n < MEM) & (n < span0 + q_span) & (n * C < length)
        same = (u // C) == q_span
        ahead = (u >= (q_span + 1) * C) & (u < (q_span + 1) * C + RC)
        in_frames = (n >= MEM) & (same | ahead) & (first_frame + u < length)
        bias[b] = jnp.where(in_memory | in_frames, 0.0, NEG_BIG)

    own_row = jnp.broadcast_to(owners[...].astype(F32), (TOK, TOK))
    own_col = own_row.T
    earlier = lax.broadcasted_iota(jnp.int32, (TOK, TOK), 0) < lax.broadcasted_iota(
        jnp.int32, (TOK, TOK), 1
    )
    slot = jnp.sum(jnp.where((own_row == own_col) & earlier, 1.0, 0.0), axis=0, keepdims=True)
    target = owners[...].astype(F32) * CAP + slot
    place = lax.broadcasted_iota(jnp.int32, (SLOTS, TOK), 0).astype(F32)
    route = jnp.where(place == target, 1.0, 0.0).astype(BF)
    member = jnp.where(
        lax.broadcasted_iota(jnp.int32, (TOK, F), 0) == segments[...], 1.0, 0.0
    ).astype(BF)
    chosen = dot_nn(route, member)
    ri[...] = chosen.astype(BF)
    cnt[...] = jnp.broadcast_to(
        jnp.maximum(jnp.sum(chosen, axis=1, keepdims=True), 1.0), (SLOTS, 128)
    )

    def gather(v):
        for i in range(n_steps):
            ring_wait(v, i, w_piece, w_send, w_recv)
            if i + 1 < n_steps:
                ring_start(v, i + 1, w_piece, w_send, w_recv)
            sib_start(v, i, w_piece, ws_send, ws_recv)
            ring_wait(v, i, m_piece, m_send, m_recv)
            if i + 1 < n_steps:
                ring_start(v, i + 1, m_piece, m_send, m_recv)
        ring_start(v, 0, o_piece, o_send, o_recv)
        for i in range(n_steps):
            sib_wait(v, i, w_piece, ws_send, ws_recv)

    per_core(gather)
    for copy in lw_first:
        copy.start()
    right.wait()

    kk[pl.ds(MEM + F, QB), :] = jnp.zeros((QB, GW), BF)
    vv[pl.ds(MEM + F, QB), :] = jnp.zeros((QB, GW), BF)
    lane_head = lax.broadcasted_iota(jnp.int32, (1, GW), 1) // (D // H)

    def out_step(v, i):
        ring_wait(v, i, o_piece, o_send, o_recv)
        if i + 1 < n_steps:
            ring_start(v, i + 1, o_piece, o_send, o_recv)
        sib_start(v, i, o_piece, os_send, os_recv)

    lw_second = [
        remote(lw_half(lw_down * 2 + c, 0), lw_half(lw_down * 2 + c, 0), l_send.at[2], l_recv.at[2], (lw_up * 2 + c, t)),
        remote(lw_half(lw_up * 2 + c, 1), lw_half(lw_up * 2 + c, 1), l_send.at[3], l_recv.at[3], (lw_down * 2 + c, t)),
        remote(lwg.at[lw_down * 2 + c], lwg.at[lw_down * 2 + c], ls_send.at[1], ls_recv.at[1], sib),
        remote(lwg.at[lw_up * 2 + c], lwg.at[lw_up * 2 + c], ls_send.at[2], ls_recv.at[2], sib),
    ]
    lw_third = remote(lwg.at[lw_far * 2 + c], lwg.at[lw_far * 2 + c], ls_send.at[3], ls_recv.at[3], sib)

    def hop(slot_ref, k):
        return remote(slot_ref, slot_ref, l_send.at[k], l_recv.at[k], sib)

    def side(slot_ref, k):
        return remote(slot_ref, slot_ref, ls_send.at[k], ls_recv.at[k], sib)

    def lw_step_two():
        hop(lwg.at[lw_down * 2 + c], 0).wait_recv()
        hop(lwg.at[lw_up * 2 + c], 1).wait_recv()
        for copy in lw_second:
            copy.start()

    def lw_step_three():
        hop(lw_half(lw_far * 2 + c, 0), 2).wait_recv()
        hop(lw_half(lw_far * 2 + c, 1), 3).wait_recv()
        lw_third.start()

    @pl.loop(0, G)
    def _(j):
        g = wrap(x + j, NX)

        @pl.loop(0, 2)
        def _(i):
            rows = pl.ds(pl.multiple_of(i * 256, 256), 256)
            a = xs[rows, :]
            q = dot_nt(a, wg[0, g].reshape(GW, D)) * (D // H) ** -0.5
            for h in range(4):
                q4[h, rows, :] = jnp.where(lane_head == h, q, 0.0).astype(BF)
            at = pl.ds(pl.multiple_of(MEM + i * 256, 256), 256)
            kk[at, :] = dot_nt(a, wg[1, g].reshape(GW, D)).astype(BF)
            vv[at, :] = dot_nt(a, wg[2, g].reshape(GW, D)).astype(BF)
            a = mg[pl.ds(2 * i, 2)].reshape(256, D)
            kk[rows, :] = dot_nt(a, wg[1, g].reshape(GW, D)).astype(BF)
            vv[rows, :] = dot_nt(a, wg[2, g].reshape(GW, D)).astype(BF)

        a = xs[pl.ds(F, 16), :]
        kk[pl.ds(MEM + F, 16), :] = dot_nt(a, wg[1, g].reshape(GW, D)).astype(BF)
        vv[pl.ds(MEM + F, 16), :] = dot_nt(a, wg[2, g].reshape(GW, D)).astype(BF)

        for jj in range(G):

            @pl.when(j == jj)
            def _():
                def one(v):
                    if jj < 3:
                        out_step(v, 2 * jj)

                per_core(one)
                if jj == 2:
                    lw_step_two()

        @pl.loop(0, F // QB)
        def _(b):
            rows = pl.ds(pl.multiple_of(b * QB, QB), QB)
            near = pl.ds(pl.multiple_of(MEM + b * QB, QB), 2 * QB)
            q = q4[:, rows, :].reshape(4 * QB, GW)
            far_keys, near_keys = kk[pl.ds(0, MEM), :], kk[near, :]
            s = jnp.concatenate([dot_nt(q, far_keys), dot_nt(q, near_keys)], axis=1)
            s = (s.reshape(4, QB, KW) + bias[b][None]).reshape(4 * QB, KW)
            peak = jnp.max(s, axis=1, keepdims=True)
            w = jnp.exp(s - peak)
            total = jnp.sum(w, axis=1, keepdims=True)
            w = w.astype(BF)
            o = dot_nn(w[:, :MEM], vv[pl.ds(0, MEM), :]) + dot_nn(w[:, MEM:], vv[near, :])
            o = (o / total).reshape(4, QB, GW)
            out = o[3]
            for h in range(3):
                out = jnp.where(lane_head == h, o[h], out)
            att[g, rows, :] = out.astype(BF)

        for jj in range(G):

            @pl.when(j == jj)
            def _():
                def two(v):
                    if jj < 3:
                        out_step(v, 2 * jj + 1)

                per_core(two)
                if jj == 3:
                    lw_step_three()

    def out_end(v):
        for i in range(n_steps):
            sib_wait(v, i, o_piece, os_send, os_recv)

    per_core(out_end)

    @pl.loop(0, F // QB)
    def _(b):
        rows = pl.ds(pl.multiple_of(b * QB, QB), QB)
        w = owg[...].reshape(D, D)
        o = dot_nt(att[0, rows, :], w[:, :GW])
        for g in range(1, G):
            o += dot_nt(att[g, rows, :], w[:, g * GW : (g + 1) * GW])
        live = first_frame + b * QB + lax.broadcasted_iota(jnp.int32, (QB, 1), 0) < length
        enc[rows, :] = jnp.where(live, frames[rows, :].astype(F32) + o, 0.0).astype(BF)

    enc_out = pltpu.make_async_copy(enc, enc_hbm, out_sem.at[0])
    enc_out.start()

    sent = dot_nn(ri[...], enc[...]) / cnt[:, :1]
    sb[...] = sent.reshape(N_TM, CAP, D).astype(BF)
    rb[t] = sb[t]

    @pl.loop(1, N_TM)
    def _(d):
        to = lax.rem(t + d, N_TM)
        remote(sb.at[to], rb.at[t], a_send.at[d], a_recv.at[d], (r, to)).start()

    side(lwg.at[r], 0).wait_send()
    for k, slot in enumerate((r, lw_down * 2 + c, lw_up * 2 + c, lw_far * 2 + c)):
        if k:
            side(lwg.at[slot], k).wait_send()
        other = lax.rem(slot, 2)
        side(lwg.at[slot + 1 - 2 * other], k).wait_recv()
    hop(lwg.at[r], 0).wait_send()
    hop(lwg.at[r], 1).wait_send()
    hop(lw_half(r, 0), 2).wait_send()
    hop(lw_half(r, 0), 3).wait_send()

    @pl.loop(1, N_TM)
    def _(d):
        to = lax.rem(t + d, N_TM)
        source = wrap(t - d, N_TM)
        copy = remote(sb.at[to], rb.at[source], a_send.at[d], a_recv.at[d], (r, to))
        copy.wait_recv()
        copy.wait_send()

    got = rb[...].astype(F32).reshape(SLOTS, D).astype(BF)
    for k in range(2 * NY):
        lmo[:, k * 256 : (k + 1) * 256] = dot_nn(got, lwg[k]).astype(BF)
    lm_out = pltpu.make_async_copy(lmo, lm_hbm, out_sem.at[1])
    lm_out.start()
    enc_out.wait()
    lm_out.wait()


def per_device(
    frames, lengths, norm_gain, memory_gain, qkv_weight, out_weight, segment_ids, owners, language_weight
):
    vmem = pl.BlockSpec(memory_space=pltpu.VMEM)
    smem = pl.BlockSpec(memory_space=pltpu.SMEM)
    hbm = pl.BlockSpec(memory_space=pl.ANY)
    dma = pltpu.SemaphoreType.DMA
    n = 12
    enc, lm = pl.pallas_call(
        kernel,
        out_shape=(
            jax.ShapeDtypeStruct((F, D), BF),
            jax.ShapeDtypeStruct((SLOTS, DL), BF),
        ),
        in_specs=[vmem, smem, vmem, vmem, hbm, hbm, vmem, vmem, hbm],
        out_specs=(hbm, hbm),
        scratch_shapes=[
            pltpu.VMEM((3, NX, NZ, 2, 16, D), BF),
            pltpu.VMEM((NX, NZ, 2, 16, D), BF),
            pltpu.VMEM((2 * NY, D, DL // (2 * NY)), BF),
            pltpu.VMEM((F + 16, D), BF),
            pltpu.VMEM((NX, NZ, 16, D), BF),
            pltpu.VMEM((F // C, D), F32),
            pltpu.VMEM((4, F, GW), BF),
            pltpu.VMEM((MEM + F + QB, GW), BF),
            pltpu.VMEM((MEM + F + QB, GW), BF),
            pltpu.VMEM((G, F, GW), BF),
            pltpu.VMEM((F // QB, QB, KW), F32),
            pltpu.VMEM((SLOTS, F), BF),
            pltpu.VMEM((SLOTS, 128), F32),
            pltpu.VMEM((F, D), BF),
            pltpu.VMEM((N_TM, CAP, D), BF),
            pltpu.VMEM((N_TM, CAP, D), BF),
            pltpu.VMEM((SLOTS, DL), BF),
            dma((n,)), dma((n,)), dma((n,)), dma((n,)), dma((n,)), dma((n,)),
            dma((n,)), dma((n,)), dma((n,)), dma((n,)),
            dma((1,)), dma((1,)), dma((4,)), dma((4,)), dma((4,)), dma((4,)),
            dma((N_TM,)), dma((N_TM,)), dma((5,)), dma((2,)),
        ],
        compiler_params=pltpu.CompilerParams(
            collective_id=0, has_side_effects=True, vmem_limit_bytes=58 * 2**20
        ),
        name="block",
    )(
        frames[0],
        lengths,
        norm_gain[None],
        memory_gain[None],
        qkv_weight.transpose(0, 2, 1),
        out_weight.T,
        segment_ids[0],
        owners[0, :, :, 0],
        language_weight,
    )
    return (enc[None], lm[None, None])


def solution(mesh):
    in_specs = (
        P("rec", "tm", None),
        P("rec"),
        P(),
        P(),
        P(None, None, "tm"),
        P(None, "tm"),
        P("rec", "tm", None),
        P("rec", "tm", None, None),
        P(None, "rec"),
    )
    out_specs = (P("rec", "tm", None), P("rec", "tm", None, None))
    return jax.shard_map(
        per_device, mesh=mesh, in_specs=in_specs, out_specs=out_specs, check_vma=False
    )
```

```python
import functools

import jax
import jax.numpy as jnp
from jax import lax
from jax.experimental import pallas as pl
from jax.experimental.pallas import tpu as pltpu
from jax.sharding import PartitionSpec as P

H = 16
C = 32
RC = 8
EPS_NORM = 1e-05
EPS_MEMORY = 1e-06
NEG_BIG = -1e30

NX, NZ, NY = 4, 8, 4
N_TM = NX * NZ
F = 512
D = 1024
DL = 2048
TOK = 128
CAP = 8
SLOTS = 256
G = 4
GW = D // G
HEAD = D // H
QB = 64
MEM = N_TM * F // C
KW = MEM + 2 * QB
NCH = 2
CH = D // NCH
LOG2E = 1.4426950408889634
BF = jnp.bfloat16
F32 = jnp.float32


def dot_nt(a, b):
    return lax.dot_general(a, b, (((1,), (1,)), ((), ())), preferred_element_type=F32)


def dot_nn(a, b):
    return lax.dot_general(a, b, (((1,), (0,)), ((), ())), preferred_element_type=F32)


def wrap(a, n):
    return lax.rem(a + 2 * n, n)


def kernel(
    frames, lengths, norm_gain, memory_gain, wq_hbm, wo_hbm, segments, owners, lw_hbm,
    enc_hbm, lm_hbm,
    wg, owg, lwg, xs, mg, mrows, q4, kk, vv, att, bias, ri, cnt, enc, sb, rb, lacc, lmo,
    zw_send, zw_recv, zm_send, zm_recv, xw_send, xw_recv, xm_send, xm_recv, sw_send, sw_recv,
    oz_send, oz_recv, ox_send, ox_recv, oy_send, oy_recv, os_send, os_recv,
    r_send, r_recv, l_send, l_recv, ls_send, ls_recv, a_send, a_recv, own_sem, out_sem,
):
    r = lax.axis_index("rec")
    t = lax.axis_index("tm")
    y, c = r // 2, lax.rem(r, 2)
    x, z = t // NZ, lax.rem(t, NZ)
    sib = (y * 2 + (1 - c), t)
    first_frame = t * F
    length = lengths[0]

    barrier = pltpu.get_barrier_semaphore()

    @pl.loop(1, N_TM)
    def _(d):
        pl.semaphore_signal(
            barrier, inc=1, device_id=(r, lax.rem(t + d, N_TM)), device_id_type=pl.DeviceIdType.MESH
        )

    @pl.loop(1, 2 * NY)
    def _(d):
        pl.semaphore_signal(
            barrier, inc=1, device_id=(lax.rem(r + d, 2 * NY), t), device_id_type=pl.DeviceIdType.MESH
        )

    pl.semaphore_wait(barrier, N_TM - 1 + 2 * NY - 1)

    def remote(src, dst, send, recv, device):
        return pltpu.make_async_remote_copy(
            src_ref=src,
            dst_ref=dst,
            send_sem=send,
            recv_sem=recv,
            device_id=device,
            device_id_type=pl.DeviceIdType.MESH,
        )

    def at_z(by):
        return (r, x * NZ + wrap(z + by, NZ))

    def at_x(by):
        return (r, wrap(x + by, NX) * NZ + z)

    def at_y(by):
        return (wrap(y + by, NY) * 2 + c, t)

    def per_core(fn):
        for v in (0, 1):
            pl.when(c == v)(functools.partial(fn, v))

    ZK = NZ // 2

    def halved(ref, k, d):
        if k < ZK:
            return ref
        return ref.at[(slice(None),) * (len(ref.shape) - 1) + (pl.ds(d * (D // 2), D // 2),)]

    def ring_start(k, piece, send, recv, base=0, own=None):
        for d, s in enumerate((1, -1)):
            dst = halved(piece(wrap(z - s * (k - 1), NZ)), k, d)
            n = base + 2 * (k - 1) + d
            remote(own if own is not None else dst, dst, send.at[n], recv.at[n], at_z(s)).start()

    def ring_wait(k, piece, send, recv, base=0):
        for d, s in enumerate((1, -1)):
            ref = halved(piece(wrap(z - s * k, NZ)), k, d)
            n = base + 2 * (k - 1) + d
            copy = remote(ref, ref, send.at[n], recv.at[n], at_z(s))
            copy.wait_recv()
            copy.wait_send()

    def arrived(k):
        return [wrap(z - k, NZ)] + ([wrap(z + k, NZ)] if k < ZK else [])

    def group(e):
        return wrap(x - e, NX)

    def w_ring(v, e):
        return lambda o: wg.at[:, group(e), o, v]

    def w_group(v, e):
        return wg.at[:, group(e), :, v]

    def m_ring(v):
        return (lambda o: mg.at[x, o]) if v == 0 else (lambda o: mg.at[:, o])

    def across_start(src, dst, send, recv, peers):
        for e in peers:
            remote(src, dst, send.at[e], recv.at[e], at_x(e)).start()

    def w_across(v, e):
        return w_group(0, e) if v == 0 else wg.at[:, group(e), z, 1]

    def m_across(v, e):
        return mg.at[group(e)] if v == 0 else mg.at[group(e), z]

    def across_wait(ref, recv, e):
        remote(ref, ref, xw_send.at[e], recv.at[e], at_x(e)).wait_recv()

    def to_sibling(v, e):
        return remote(w_group(v, e), w_group(v, e), sw_send.at[e], sw_recv.at[e], sib)

    def from_sibling(e):
        def wait(v):
            to_sibling(1 - v, e).wait_recv()

        per_core(wait)

    lanes = pl.ds(pl.multiple_of(r * 128, 128), 128)

    def first_hop(v):
        own = wq_hbm.at[:, pl.ds(16 * v, 16)]
        ring_start(1, w_ring(v, 0), zw_send, zw_recv, own=own)
        across_start(own, wg.at[:, x, z, v], xw_send, xw_recv, (1, 3) if v == 0 else (1, 3, 2))

    per_core(first_hop)
    own_copies = [
        pltpu.make_async_copy(
            wq_hbm.at[:, pl.ds(pl.multiple_of(16 * c, 16), 16)], wg.at[:, x, z, c], own_sem.at[0]
        ),
        pltpu.make_async_copy(wo_hbm.at[:, lanes], owg.at[x, z, :, lanes], own_sem.at[1]),
        pltpu.make_async_copy(lw_hbm, lwg.at[r], own_sem.at[2]),
    ]
    for copy in own_copies:
        copy.start()

    gain = norm_gain[...]

    @pl.loop(0, F // C)
    def _(i):
        rows = pl.ds(pl.multiple_of(i * C, C), C)
        v = frames[rows, :].astype(F32)
        centred = v - jnp.mean(v, axis=1, keepdims=True)
        spread = jnp.mean(centred * centred, axis=1, keepdims=True)
        normed = (centred * lax.rsqrt(spread + EPS_NORM) * gain).astype(BF)
        xs[rows, :] = normed
        start = first_frame + i * C
        live = start + lax.broadcasted_iota(jnp.int32, (C, 1), 0) < length
        total = jnp.sum(jnp.where(live, normed.astype(F32), 0.0), axis=0, keepdims=True)
        count = jnp.clip(length - start, 1, C).astype(F32)
        mrows[pl.ds(i, 1), :] = total / count

    means = mrows[...]
    power = jnp.mean(means * means, axis=1, keepdims=True)
    mg[x, z] = (means * lax.rsqrt(power + EPS_MEMORY) * memory_gain[...]).astype(BF)

    def memory_hop(v):
        across_start(mg.at[x, z], mg.at[x, z], xm_send, xm_recv, (1, 3, 2))
        if v == 0:
            ring_start(1, m_ring(v), zm_send, zm_recv)
        else:
            for e in (1, 3, 2):
                across_wait(m_across(1, e), xm_recv, e)
            ring_start(1, m_ring(v), zm_send, zm_recv)

    per_core(memory_hop)

    right = remote(
        xs.at[pl.ds(0, 16)], xs.at[pl.ds(F, 16)], r_send.at[0], r_recv.at[0], (r, wrap(t - 1, N_TM))
    )
    right.start()
    for copy in own_copies:
        copy.wait()

    def o_z(o):
        return owg.at[x, o, :, lanes]

    def o_x(e):
        return owg.at[group(e), :, :, lanes]

    def o_y(by, core):
        return owg.at[:, :, :, pl.ds(pl.multiple_of((wrap(y - by, NY) * 2 + core) * 128, 128), 128)]

    for d in range(1, NZ):
        remote(o_z(z), o_z(z), oz_send.at[d], oz_recv.at[d], at_z(d)).start()

    def out_across():
        for d in range(1, NZ):
            ref = o_z(wrap(z - d, NZ))
            remote(ref, ref, oz_send.at[d], oz_recv.at[d], at_z(d)).wait_recv()
        for e in (1, 3, 2):
            remote(o_x(0), o_x(0), ox_send.at[e], ox_recv.at[e], at_x(e)).start()

    def out_up():
        for e in (1, 3, 2):
            remote(o_x(e), o_x(e), ox_send.at[e], ox_recv.at[e], at_x(e)).wait_recv()
        for by in (1, 3, 2):
            remote(o_y(0, c), o_y(0, c), oy_send.at[by], oy_recv.at[by], at_y(by)).start()
        remote(o_y(0, c), o_y(0, c), os_send.at[0], os_recv.at[0], sib).start()

    def out_side():
        for by in (1, 3, 2):
            ref = o_y(by, c)
            remote(ref, ref, oy_send.at[by], oy_recv.at[by], at_y(by)).wait_recv()
            remote(ref, ref, os_send.at[by], os_recv.at[by], sib).start()

    def out_end():
        for by in range(NY):
            ref = o_y(by, 1 - c)
            remote(ref, ref, os_send.at[by], os_recv.at[by], sib).wait_recv()

    lw_up, lw_down, lw_far = (wrap(y + k, NY) * 2 + c for k in (1, -1, 2))

    def lw_half(slot, d):
        return lwg.at[slot, pl.ds(d * (D // 2), D // 2)]

    def hop(ref, k, device=sib):
        return remote(ref, ref, l_send.at[k], l_recv.at[k], device)

    def side(ref, k):
        return remote(ref, ref, ls_send.at[k], ls_recv.at[k], sib)

    hop(lwg.at[r], 0, at_y(1)).start()
    hop(lwg.at[r], 1, at_y(-1)).start()
    side(lwg.at[r], 0).start()

    def lw_step_two():
        hop(lwg.at[lw_down], 0).wait_recv()
        hop(lwg.at[lw_up], 1).wait_recv()
        hop(lw_half(lw_down, 0), 2, at_y(1)).start()
        hop(lw_half(lw_up, 1), 3, at_y(-1)).start()
        side(lwg.at[lw_down], 1).start()
        side(lwg.at[lw_up], 2).start()

    def lw_step_three():
        hop(lw_half(lw_far, 0), 2).wait_recv()
        hop(lw_half(lw_far, 1), 3).wait_recv()
        side(lwg.at[lw_far], 3).start()

    span0 = t * (F // C)

    @pl.loop(0, F // QB)
    def _(b):
        q = b * QB + lax.broadcasted_iota(jnp.int32, (QB, KW), 0)
        n = lax.broadcasted_iota(jnp.int32, (QB, KW), 1)
        q_span = q // C
        u = b * QB + n - MEM
        in_memory = (n < MEM) & (n < span0 + q_span) & (n * C < length)
        same = (u // C) == q_span
        ahead = (u >= (q_span + 1) * C) & (u < (q_span + 1) * C + RC)
        in_frames = (n >= MEM) & (same | ahead) & (first_frame + u < length)
        bias[b] = jnp.where(in_memory | in_frames, 0.0, NEG_BIG)

    own_row = jnp.broadcast_to(owners[...].astype(F32), (TOK, TOK))
    own_col = own_row.T
    earlier = lax.broadcasted_iota(jnp.int32, (TOK, TOK), 0) < lax.broadcasted_iota(
        jnp.int32, (TOK, TOK), 1
    )
    slot = jnp.sum(jnp.where((own_row == own_col) & earlier, 1.0, 0.0), axis=0, keepdims=True)
    target = owners[...].astype(F32) * CAP + slot
    place = lax.broadcasted_iota(jnp.int32, (SLOTS, TOK), 0).astype(F32)
    route = jnp.where(place == target, 1.0, 0.0).astype(BF)
    member = jnp.where(
        lax.broadcasted_iota(jnp.int32, (TOK, F), 0) == segments[...], 1.0, 0.0
    ).astype(BF)
    chosen = dot_nn(route, member)
    ri[...] = chosen.astype(BF)
    cnt[...] = jnp.broadcast_to(
        jnp.maximum(jnp.sum(chosen, axis=1, keepdims=True), 1.0), (SLOTS, 128)
    )
    kk[pl.ds(MEM + F, QB), :] = jnp.zeros((QB, GW), BF)
    vv[pl.ds(MEM + F, QB), :] = jnp.zeros((QB, GW), BF)

    def gather(v):
        for k in range(1, ZK + 1):
            ring_wait(k, w_ring(v, 0), zw_send, zw_recv)
            if k < ZK:
                ring_start(k + 1, w_ring(v, 0), zw_send, zw_recv)
            if v == 0:
                for o in arrived(k):
                    across_start(w_ring(0, 0)(o), w_ring(0, 0)(o), xw_send, xw_recv, (1, 3))
            ring_wait(k, m_ring(v), zm_send, zm_recv)
            if k < ZK:
                ring_start(k + 1, m_ring(v), zm_send, zm_recv)
            if v == 0:
                for o in arrived(k):
                    across_start(mg.at[x, o], mg.at[x, o], xm_send, xm_recv, (1, 3, 2))
            if v == 1 and k == 1:
                for e in (1, 3, 2):
                    across_wait(w_across(1, e), xw_recv, e)
                b_start(1, 1)
                b_start(3, 1)
            if v == 1 and k >= 2:
                b_next(1, k - 1)
                b_next(3, k - 1)
        to_sibling(v, 0).start()
        if v == 0:
            across_start(w_group(0, 0), w_group(0, 0), xw_send, xw_recv, (2,))
            for e in (1, 3, 2):
                across_wait(m_across(0, e), xm_recv, e)

    def b_start(e, k):
        ring_start(k, w_ring(1, e), zw_send, zw_recv, base=8 * e)

    def b_next(e, k):
        ring_wait(k, w_ring(1, e), zw_send, zw_recv, base=8 * e)
        if k < ZK:
            b_start(e, k + 1)
        else:
            to_sibling(1, e).start()

    def x_next(e):
        across_wait(w_across(0, e), xw_recv, e)
        to_sibling(0, e).start()

    per_core(gather)
    out_across()
    lw_step_two()
    right.wait()

    def hook_0q(v):
        if v == 1:
            b_next(1, 4)
            b_next(3, 4)
            b_start(2, 1)
        else:
            x_next(1)

    def hook_0a(v):
        if v == 1:
            b_next(2, 1)
        else:
            x_next(3)

    def hook_1q(v):
        if v == 1:
            b_next(2, 2)

    def hook_1a(v):
        if v == 1:
            b_next(2, 3)

    def hook_2q(v):
        if v == 1:
            b_next(2, 4)
        else:
            x_next(2)

    def after_projection(j):
        @pl.when(j == 0)
        def _():
            per_core(hook_0q)

        @pl.when(j == 1)
        def _():
            per_core(hook_1q)

        @pl.when(j == 2)
        def _():
            per_core(hook_2q)

        @pl.when(j == 3)
        def _():
            out_side()

    def after_attention(j):
        @pl.when(j == 0)
        def _():
            per_core(hook_0a)
            out_up()

        @pl.when(j == 1)
        def _():
            per_core(hook_1a)
            lw_step_three()

    lane_head = lax.broadcasted_iota(jnp.int32, (1, GW), 1) // HEAD

    @pl.loop(0, G)
    def _(j):
        for jj, e in enumerate((0, 1, 3, 2)):
            pl.when(j == jj)(functools.partial(from_sibling, e))
        g = wrap(x - (j + (j // 2) * (5 - 2 * j)), NX)
        a = xs[...]
        q = dot_nt(a, wg[0, g].reshape(GW, D))[:F] * (HEAD**-0.5 * LOG2E)
        for h in range(4):
            q4[:, h * QB : (h + 1) * QB, :] = (
                jnp.where(lane_head == h, q, 0.0).astype(BF).reshape(F // QB, QB, GW)
            )
        m = mg[...].reshape(MEM, D)
        for n, ref in ((1, kk), (2, vv)):
            w = wg[n, g].reshape(GW, D)
            ref[pl.ds(MEM, F + 16), :] = dot_nt(a, w).astype(BF)
            ref[pl.ds(0, MEM), :] = dot_nt(m, w).astype(BF)
        after_projection(j)
        columns = pl.ds(pl.multiple_of(g * GW, GW), GW)
        for b in range(F // QB):
            near = pl.ds(MEM + b * QB, 2 * QB)
            q = q4[b]
            s = jnp.concatenate([dot_nt(q, kk[pl.ds(0, MEM), :]), dot_nt(q, kk[near, :])], axis=1)
            s = (s.reshape(4, QB, KW) + bias[b][None]).reshape(4 * QB, KW)
            peak = jnp.max(s, axis=1, keepdims=True)
            w = jnp.exp2(s - peak)
            total = jnp.sum(w, axis=1, keepdims=True)
            w = w.astype(BF)
            o = dot_nn(w[:, :MEM], vv[pl.ds(0, MEM), :]) + dot_nn(w[:, MEM:], vv[near, :])
            o, total = o.reshape(4, QB, GW), total.reshape(4, QB, 1)
            out, den = o[3], jnp.broadcast_to(total[3], (QB, GW))
            for h in range(3):
                out = jnp.where(lane_head == h, o[h], out)
                den = jnp.where(lane_head == h, total[h], den)
            att[b * QB : (b + 1) * QB, columns] = (out / den).astype(BF)
        after_attention(j)

    out_end()

    for ch in range(NCH):
        features = slice(ch * CH, (ch + 1) * CH)
        w = owg[pl.ds(ch * (NX // NCH), NX // NCH)].reshape(CH, D)
        for b in range(2):
            rows = slice(b * 256, (b + 1) * 256)
            o = dot_nt(att[rows, :], w)
            live = first_frame + b * 256 + lax.broadcasted_iota(jnp.int32, (256, 1), 0) < length
            enc[rows, features] = jnp.where(
                live, frames[rows, features].astype(F32) + o, 0.0
            ).astype(BF)
        sent = dot_nn(ri[...], enc[:, features]) / cnt[:, :1]
        sb[ch] = sent.reshape(N_TM, CAP, CH).astype(BF)

        @pl.loop(1, N_TM)
        def _(d):
            to = lax.rem(t + d, N_TM)
            remote(sb.at[ch, to], rb.at[ch, t], a_send.at[ch, d], a_recv.at[ch, d], (r, to)).start()

        rb[ch, t] = sb[ch, t]

    enc_out = pltpu.make_async_copy(enc, enc_hbm, out_sem.at[0])
    enc_out.start()

    def sent_core(v):
        for e in (1, 2, 3):
            ref = w_group(0, 0) if v == 0 else wg.at[:, x, z, 1]
            remote(ref, ref, xw_send.at[e], xw_recv.at[e], sib).wait_send()
            ref = mg.at[x] if v == 0 else mg.at[x, z]
            remote(ref, ref, xm_send.at[e], xm_recv.at[e], sib).wait_send()
        for e in range(NX):
            to_sibling(v, e).wait_send()

    per_core(sent_core)
    for d in range(1, NZ):
        remote(o_z(z), o_z(z), oz_send.at[d], oz_recv.at[d], sib).wait_send()
    for e in (1, 2, 3):
        remote(o_x(0), o_x(0), ox_send.at[e], ox_recv.at[e], sib).wait_send()
        remote(o_y(0, c), o_y(0, c), oy_send.at[e], oy_recv.at[e], sib).wait_send()
    for by in range(NY):
        ref = o_y(by, c)
        remote(ref, ref, os_send.at[by], os_recv.at[by], sib).wait_send()
    for k, slot in enumerate((r, lw_down, lw_up, lw_far)):
        side(lwg.at[slot], k).wait_send()
        side(lwg.at[slot + 1 - 2 * c], k).wait_recv()
    hop(lwg.at[r], 0).wait_send()
    hop(lwg.at[r], 1).wait_send()
    hop(lw_half(r, 0), 2).wait_send()
    hop(lw_half(r, 0), 3).wait_send()

    for ch in range(NCH):

        @pl.loop(1, N_TM)
        def _(d):
            to = lax.rem(t + d, N_TM)
            source = wrap(t - d, N_TM)
            copy = remote(
                sb.at[ch, to], rb.at[ch, source], a_send.at[ch, d], a_recv.at[ch, d], (r, to)
            )
            copy.wait_recv()
            copy.wait_send()

        got = rb[ch].astype(F32).reshape(SLOTS, CH).astype(BF)
        for k in range(2 * NY):
            part = dot_nn(got, lwg[k, ch * CH : (ch + 1) * CH, :])
            if ch > 0:
                part += lacc[k]
            if ch < NCH - 1:
                lacc[k] = part
            else:
                lmo[:, k * 256 : (k + 1) * 256] = part.astype(BF)
    lm_out = pltpu.make_async_copy(lmo, lm_hbm, out_sem.at[1])
    lm_out.start()
    enc_out.wait()
    lm_out.wait()


def per_device(
    frames, lengths, norm_gain, memory_gain, qkv_weight, out_weight, segment_ids, owners, language_weight
):
    vmem = pl.BlockSpec(memory_space=pltpu.VMEM)
    smem = pl.BlockSpec(memory_space=pltpu.SMEM)
    hbm = pl.BlockSpec(memory_space=pl.ANY)
    dma = pltpu.SemaphoreType.DMA
    enc, lm = pl.pallas_call(
        kernel,
        out_shape=(
            jax.ShapeDtypeStruct((F, D), BF),
            jax.ShapeDtypeStruct((SLOTS, DL), BF),
        ),
        in_specs=[vmem, smem, vmem, vmem, hbm, hbm, vmem, vmem, hbm],
        out_specs=(hbm, hbm),
        scratch_shapes=[
            pltpu.VMEM((3, NX, NZ, 2, 16, D), BF),
            pltpu.VMEM((NX, NZ, 32, D), BF),
            pltpu.VMEM((2 * NY, D, DL // (2 * NY)), BF),
            pltpu.VMEM((F + 16, D), BF),
            pltpu.VMEM((NX, NZ, 16, D), BF),
            pltpu.VMEM((F // C, D), F32),
            pltpu.VMEM((F // QB, 4 * QB, GW), BF),
            pltpu.VMEM((MEM + F + QB, GW), BF),
            pltpu.VMEM((MEM + F + QB, GW), BF),
            pltpu.VMEM((F, D), BF),
            pltpu.VMEM((F // QB, QB, KW), F32),
            pltpu.VMEM((SLOTS, F), BF),
            pltpu.VMEM((SLOTS, 128), F32),
            pltpu.VMEM((F, D), BF),
            pltpu.VMEM((NCH, N_TM, CAP, CH), BF),
            pltpu.VMEM((NCH, N_TM, CAP, CH), BF),
            pltpu.VMEM((2 * NY, SLOTS, 256), F32),
            pltpu.VMEM((SLOTS, DL), BF),
            dma((32,)), dma((32,)), dma((8,)), dma((8,)), dma((4,)), dma((4,)), dma((4,)), dma((4,)),
            dma((4,)), dma((4,)),
            dma((8,)), dma((8,)), dma((4,)), dma((4,)), dma((4,)), dma((4,)), dma((4,)), dma((4,)),
            dma((1,)), dma((1,)), dma((4,)), dma((4,)), dma((4,)), dma((4,)),
            dma((NCH, N_TM)), dma((NCH, N_TM)), dma((3,)), dma((2,)),
        ],
        compiler_params=pltpu.CompilerParams(
            collective_id=0, has_side_effects=True, vmem_limit_bytes=58 * 2**20
        ),
        name="block",
    )(
        frames[0],
        lengths,
        norm_gain[None],
        memory_gain[None],
        qkv_weight.transpose(0, 2, 1),
        out_weight.T,
        segment_ids[0],
        owners[0, :, :, 0],
        language_weight,
    )
    return (enc[None], lm[None, None])


def solution(mesh):
    in_specs = (
        P("rec", "tm", None),
        P("rec"),
        P(),
        P(),
        P(None, None, "tm"),
        P(None, "tm"),
        P("rec", "tm", None),
        P("rec", "tm", None, None),
        P(None, "rec"),
    )
    out_specs = (P("rec", "tm", None), P("rec", "tm", None, None))
    return jax.shard_map(
        per_device, mesh=mesh, in_specs=in_specs, out_specs=out_specs, check_vma=False
    )
```

```python
import functools

import jax
import jax.numpy as jnp
from jax import lax
from jax.experimental import pallas as pl
from jax.experimental.pallas import tpu as pltpu
from jax.sharding import PartitionSpec as P

H = 16
C = 32
RC = 8
EPS_NORM = 1e-05
EPS_MEMORY = 1e-06
NEG_BIG = -1e30

NX, NZ, NY = 4, 8, 4
N_TM = NX * NZ
F = 512
D = 1024
DL = 2048
TOK = 128
CAP = 8
SLOTS = 256
G = 4
GW = D // G
HEAD = D // H
QB = 64
MEM = N_TM * F // C
KW = MEM + 2 * QB
NCH = 2
CH = D // NCH
LOG2E = 1.4426950408889634
BF = jnp.bfloat16
F32 = jnp.float32


def dot_nt(a, b):
    return lax.dot_general(a, b, (((1,), (1,)), ((), ())), preferred_element_type=F32)


def dot_nn(a, b):
    return lax.dot_general(a, b, (((1,), (0,)), ((), ())), preferred_element_type=F32)


def wrap(a, n):
    return lax.rem(a + 2 * n, n)


def kernel(
    frames, lengths, norm_gain, memory_gain, wq_hbm, wo_hbm, segments, owners, lw_hbm,
    enc_hbm, lm_hbm,
    wg, owg, lwg, xs, mg, mrows, q4, kk, vv, att, bias, ri, cnt, enc, sb, rb, lacc, lmo,
    zw_send, zw_recv, zm_send, zm_recv, xw_send, xw_recv, xm_send, xm_recv, sw_send, sw_recv,
    x2_send, x2_recv, z2_send, z2_recv, y2_send, y2_recv, s2_send, s2_recv,
    oz_send, oz_recv, ox_send, ox_recv, oy_send, oy_recv, os_send, os_recv,
    r_send, r_recv, l_send, l_recv, ls_send, ls_recv, a_send, a_recv, own_sem, out_sem,
):
    r = lax.axis_index("rec")
    t = lax.axis_index("tm")
    y, c = r // 2, lax.rem(r, 2)
    x, z = t // NZ, lax.rem(t, NZ)
    sib = (y * 2 + (1 - c), t)
    first_frame = t * F
    length = lengths[0]

    barrier = pltpu.get_barrier_semaphore()

    @pl.loop(1, N_TM)
    def _(d):
        pl.semaphore_signal(
            barrier, inc=1, device_id=(r, lax.rem(t + d, N_TM)), device_id_type=pl.DeviceIdType.MESH
        )

    @pl.loop(1, 2 * NY)
    def _(d):
        pl.semaphore_signal(
            barrier, inc=1, device_id=(lax.rem(r + d, 2 * NY), t), device_id_type=pl.DeviceIdType.MESH
        )

    pl.semaphore_wait(barrier, N_TM - 1 + 2 * NY - 1)

    def remote(src, dst, send, recv, device):
        return pltpu.make_async_remote_copy(
            src_ref=src,
            dst_ref=dst,
            send_sem=send,
            recv_sem=recv,
            device_id=device,
            device_id_type=pl.DeviceIdType.MESH,
        )

    def at_z(by):
        return (r, x * NZ + wrap(z + by, NZ))

    def at_x(by):
        return (r, wrap(x + by, NX) * NZ + z)

    def at_y(by):
        return (wrap(y + by, NY) * 2 + c, t)

    def per_core(fn):
        for v in (0, 1):
            pl.when(c == v)(functools.partial(fn, v))

    ZK = NZ // 2

    def halved(ref, k, d):
        if k < ZK:
            return ref
        return ref.at[(slice(None),) * (len(ref.shape) - 1) + (pl.ds(d * (D // 2), D // 2),)]

    def ring_start(k, piece, send, recv, own=None):
        for d, s in enumerate((1, -1)):
            dst = halved(piece(wrap(z - s * (k - 1), NZ)), k, d)
            n = 2 * (k - 1) + d
            remote(own if own is not None else dst, dst, send.at[n], recv.at[n], at_z(s)).start()

    def ring_wait(k, piece, send, recv):
        for d, s in enumerate((1, -1)):
            ref = halved(piece(wrap(z - s * k, NZ)), k, d)
            n = 2 * (k - 1) + d
            copy = remote(ref, ref, send.at[n], recv.at[n], at_z(s))
            copy.wait_recv()
            copy.wait_send()

    def arrived(k):
        return [wrap(z - k, NZ)] + ([wrap(z + k, NZ)] if k < ZK else [])

    def group(e):
        return wrap(x - e, NX)

    def w_ring(v, e):
        return lambda o: wg.at[:, group(e), o, v]

    def w_group(v, e):
        return wg.at[:, group(e), :, v]

    def m_ring(v):
        return (lambda o: mg.at[x, o]) if v == 0 else (lambda o: mg.at[:, o])

    def across_start(src, dst, send, recv, peers):
        for e in peers:
            remote(src, dst, send.at[e], recv.at[e], at_x(e)).start()

    def w_across(v, e):
        return w_group(v, e)

    def m_across(v, e):
        return mg.at[group(e)] if v == 0 else mg.at[group(e), z]

    def across_wait(ref, recv, e):
        remote(ref, ref, xw_send.at[e], recv.at[e], at_x(e)).wait_recv()

    def to_sibling(v, e):
        return remote(w_group(v, e), w_group(v, e), sw_send.at[e], sw_recv.at[e], sib)

    def from_sibling(e):
        def wait(v):
            to_sibling(1 - v, e).wait_recv()

        per_core(wait)

    lanes = pl.ds(pl.multiple_of(r * 128, 128), 128)

    def first_hop(v):
        own = wq_hbm.at[:, v]
        ring_start(1, w_ring(v, 0), zw_send, zw_recv, own=own)
        across_start(own, wg.at[:, x, z, v], xw_send, xw_recv, (1, 3))

    per_core(first_hop)
    far_first = remote(
        wq_hbm.at[:, :, :, lanes], wg.at[:, x, z, :, :, lanes], x2_send.at[0], x2_recv.at[0], at_x(2)
    )
    far_first.start()
    own_copies = [
        pltpu.make_async_copy(
            wq_hbm.at[:, c], wg.at[:, x, z, c], own_sem.at[0]
        ),
        pltpu.make_async_copy(wo_hbm.at[:, lanes], owg.at[x, z, :, lanes], own_sem.at[1]),
        pltpu.make_async_copy(lw_hbm, lwg.at[r], own_sem.at[2]),
    ]
    for copy in own_copies:
        copy.start()

    gain = norm_gain[...]

    @pl.loop(0, F // C)
    def _(i):
        rows = pl.ds(pl.multiple_of(i * C, C), C)
        v = frames[rows, :].astype(F32)
        centred = v - jnp.mean(v, axis=1, keepdims=True)
        spread = jnp.mean(centred * centred, axis=1, keepdims=True)
        normed = (centred * lax.rsqrt(spread + EPS_NORM) * gain).astype(BF)
        xs[rows, :] = normed
        start = first_frame + i * C
        live = start + lax.broadcasted_iota(jnp.int32, (C, 1), 0) < length
        total = jnp.sum(jnp.where(live, normed.astype(F32), 0.0), axis=0, keepdims=True)
        count = jnp.clip(length - start, 1, C).astype(F32)
        mrows[pl.ds(i, 1), :] = total / count

    means = mrows[...]
    power = jnp.mean(means * means, axis=1, keepdims=True)
    mg[x, z] = (means * lax.rsqrt(power + EPS_MEMORY) * memory_gain[...]).astype(BF)

    def round_one(v):
        ring_next(v, 1)
        across_start(mg.at[x, z], mg.at[x, z], xm_send, xm_recv, (1, 3, 2))
        if v == 0:
            ring_start(1, m_ring(v), zm_send, zm_recv)

    def ring_next(v, k):
        ring_wait(k, w_ring(v, 0), zw_send, zw_recv)
        if k < ZK:
            ring_start(k + 1, w_ring(v, 0), zw_send, zw_recv)
        else:
            to_sibling(v, 0).start()
        for o in arrived(k):
            across_start(w_ring(v, 0)(o), w_ring(v, 0)(o), xw_send, xw_recv, (1, 3))

    def memory_next(v, k):
        ring_wait(k, m_ring(v), zm_send, zm_recv)
        if k < ZK:
            ring_start(k + 1, m_ring(v), zm_send, zm_recv)
        if v == 0:
            for o in arrived(k):
                across_start(mg.at[x, o], mg.at[x, o], xm_send, xm_recv, (1, 3, 2))

    for copy in own_copies:
        copy.wait()
    per_core(round_one)

    right = remote(
        xs.at[pl.ds(0, 16)], xs.at[pl.ds(F, 16)], r_send.at[0], r_recv.at[0], (r, wrap(t - 1, N_TM))
    )
    right.start()

    def o_z(o):
        return owg.at[x, o, :, lanes]

    def o_x(e):
        return owg.at[group(e), :, :, lanes]

    def o_y(by, core):
        return owg.at[:, :, :, pl.ds(pl.multiple_of((wrap(y - by, NY) * 2 + core) * 128, 128), 128)]

    for d in range(1, NZ):
        remote(o_z(z), o_z(z), oz_send.at[d], oz_recv.at[d], at_z(d)).start()

    def out_across():
        for d in range(1, NZ):
            ref = o_z(wrap(z - d, NZ))
            remote(ref, ref, oz_send.at[d], oz_recv.at[d], at_z(d)).wait_recv()
        for e in (1, 3, 2):
            remote(o_x(0), o_x(0), ox_send.at[e], ox_recv.at[e], at_x(e)).start()

    def out_up():
        for e in (1, 3, 2):
            remote(o_x(e), o_x(e), ox_send.at[e], ox_recv.at[e], at_x(e)).wait_recv()
        for by in (1, 3, 2):
            remote(o_y(0, c), o_y(0, c), oy_send.at[by], oy_recv.at[by], at_y(by)).start()
        remote(o_y(0, c), o_y(0, c), os_send.at[0], os_recv.at[0], sib).start()

    def out_side():
        for by in (1, 3, 2):
            ref = o_y(by, c)
            remote(ref, ref, oy_send.at[by], oy_recv.at[by], at_y(by)).wait_recv()
            remote(ref, ref, os_send.at[by], os_recv.at[by], sib).start()

    def out_end():
        for by in range(NY):
            ref = o_y(by, 1 - c)
            remote(ref, ref, os_send.at[by], os_recv.at[by], sib).wait_recv()

    lw_up, lw_down, lw_far = (wrap(y + k, NY) * 2 + c for k in (1, -1, 2))

    def lw_half(slot, d):
        return lwg.at[slot, pl.ds(d * (D // 2), D // 2)]

    def hop(ref, k, device=sib):
        return remote(ref, ref, l_send.at[k], l_recv.at[k], device)

    def side(ref, k):
        return remote(ref, ref, ls_send.at[k], ls_recv.at[k], sib)

    hop(lwg.at[r], 0, at_y(1)).start()
    hop(lwg.at[r], 1, at_y(-1)).start()
    side(lwg.at[r], 0).start()

    def lw_step_two():
        hop(lwg.at[lw_down], 0).wait_recv()
        hop(lwg.at[lw_up], 1).wait_recv()
        hop(lw_half(lw_down, 0), 2, at_y(1)).start()
        hop(lw_half(lw_up, 1), 3, at_y(-1)).start()
        side(lwg.at[lw_down], 1).start()
        side(lwg.at[lw_up], 2).start()

    def lw_step_three():
        hop(lw_half(lw_far, 0), 2).wait_recv()
        hop(lw_half(lw_far, 1), 3).wait_recv()
        side(lwg.at[lw_far], 3).start()

    span0 = t * (F // C)

    @pl.loop(0, F // QB)
    def _(b):
        q = b * QB + lax.broadcasted_iota(jnp.int32, (QB, KW), 0)
        n = lax.broadcasted_iota(jnp.int32, (QB, KW), 1)
        q_span = q // C
        u = b * QB + n - MEM
        in_memory = (n < MEM) & (n < span0 + q_span) & (n * C < length)
        same = (u // C) == q_span
        ahead = (u >= (q_span + 1) * C) & (u < (q_span + 1) * C + RC)
        in_frames = (n >= MEM) & (same | ahead) & (first_frame + u < length)
        bias[b] = jnp.where(in_memory | in_frames, 0.0, NEG_BIG)

    own_row = jnp.broadcast_to(owners[...].astype(F32), (TOK, TOK))
    own_col = own_row.T
    earlier = lax.broadcasted_iota(jnp.int32, (TOK, TOK), 0) < lax.broadcasted_iota(
        jnp.int32, (TOK, TOK), 1
    )
    slot = jnp.sum(jnp.where((own_row == own_col) & earlier, 1.0, 0.0), axis=0, keepdims=True)
    target = owners[...].astype(F32) * CAP + slot
    place = lax.broadcasted_iota(jnp.int32, (SLOTS, TOK), 0).astype(F32)
    route = jnp.where(place == target, 1.0, 0.0).astype(BF)
    member = jnp.where(
        lax.broadcasted_iota(jnp.int32, (TOK, F), 0) == segments[...], 1.0, 0.0
    ).astype(BF)
    chosen = dot_nn(route, member)
    ri[...] = chosen.astype(BF)
    cnt[...] = jnp.broadcast_to(
        jnp.maximum(jnp.sum(chosen, axis=1, keepdims=True), 1.0), (SLOTS, 128)
    )
    kk[pl.ds(MEM + F, QB), :] = jnp.zeros((QB, GW), BF)
    vv[pl.ds(MEM + F, QB), :] = jnp.zeros((QB, GW), BF)

    def round_two(v):
        if v == 1:
            for e in (1, 3, 2):
                across_wait(m_across(1, e), xm_recv, e)
            ring_start(1, m_ring(v), zm_send, zm_recv)
        else:
            memory_next(v, 1)
        ring_next(v, 2)

    def round_three(v):
        if v == 1:
            memory_next(v, 1)
            ring_next(v, 3)
        else:
            ring_next(v, 3)
            memory_next(v, 2)

    def round_four(v):
        if v == 1:
            memory_next(v, 2)
            ring_next(v, 4)
        else:
            ring_next(v, 4)
            memory_next(v, 3)

    def round_five(v):
        memory_next(v, 3 if v == 1 else 4)

    def round_six(v):
        if v == 1:
            memory_next(v, 4)
        else:
            for e in (1, 3, 2):
                across_wait(m_across(0, e), xm_recv, e)

    def x_next(e):
        def one(v):
            across_wait(w_across(v, e), xw_recv, e)
            to_sibling(v, e).start()

        per_core(one)

    def far_piece(rec):
        return wg.at[:, group(2), :, :, :, pl.ds(pl.multiple_of(rec * 128, 128), 128)]

    def far_z(o):
        return wg.at[:, group(2), o, :, :, lanes]

    def far_along():
        remote(far_z(z), far_z(z), x2_send.at[0], x2_recv.at[0], at_x(2)).wait_recv()
        for d in (4, 3, 5, 2, 6, 1, 7):
            remote(far_z(z), far_z(z), z2_send.at[d], z2_recv.at[d], at_z(d)).start()

    def far_up():
        for d in range(1, NZ):
            ref = far_z(wrap(z - d, NZ))
            remote(ref, ref, z2_send.at[d], z2_recv.at[d], at_z(d)).wait_recv()
        ref = far_piece(r)
        for by in (1, 3, 2):
            remote(ref, ref, y2_send.at[by], y2_recv.at[by], at_y(by)).start()
        remote(ref, ref, s2_send.at[0], s2_recv.at[0], sib).start()

    def far_side():
        for by in (1, 3, 2):
            ref = far_piece(wrap(y - by, NY) * 2 + c)
            remote(ref, ref, y2_send.at[by], y2_recv.at[by], at_y(by)).wait_recv()
            remote(ref, ref, s2_send.at[by], s2_recv.at[by], sib).start()

    def far_end():
        for by in range(NY):
            ref = far_piece(wrap(y - by, NY) * 2 + 1 - c)
            remote(ref, ref, s2_send.at[by], s2_recv.at[by], sib).wait_recv()

    per_core(round_two)
    out_across()
    per_core(round_three)
    per_core(round_four)
    out_up()
    far_along()
    per_core(round_five)
    from_sibling(0)
    right.wait()
    lane_head = lax.broadcasted_iota(jnp.int32, (1, GW), 1) // HEAD

    def project_frames(g):
        a = xs[...]
        q = dot_nt(a, wg[0, g].reshape(GW, D))[:F] * (HEAD**-0.5 * LOG2E)
        for h in range(4):
            q4[:, h * QB : (h + 1) * QB, :] = (
                jnp.where(lane_head == h, q, 0.0).astype(BF).reshape(F // QB, QB, GW)
            )
        for n, ref in ((1, kk), (2, vv)):
            ref[pl.ds(MEM, F + 16), :] = dot_nt(a, wg[n, g].reshape(GW, D)).astype(BF)

    project_frames(x)
    per_core(round_six)

    def before_projection(j):
        @pl.when(j == 1)
        def _():
            from_sibling(1)

        @pl.when(j == 2)
        def _():
            from_sibling(3)

        @pl.when(j == 3)
        def _():
            far_end()

    def after_projection(j):
        @pl.when(j == 0)
        def _():
            x_next(1)
            far_up()

        @pl.when(j == 1)
        def _():
            out_side()

        @pl.when(j == 3)
        def _():
            lw_step_two()

    def after_attention(j):
        @pl.when(j == 0)
        def _():
            x_next(3)

        @pl.when(j == 2)
        def _():
            far_side()

    @pl.loop(0, G)
    def _(j):
        before_projection(j)
        g = wrap(x - (j + (j // 2) * (5 - 2 * j)), NX)

        @pl.when(j > 0)
        def _():
            project_frames(g)

        m = mg[...].reshape(MEM, D)
        for n, ref in ((1, kk), (2, vv)):
            ref[pl.ds(0, MEM), :] = dot_nt(m, wg[n, g].reshape(GW, D)).astype(BF)
        after_projection(j)
        columns = pl.ds(pl.multiple_of(g * GW, GW), GW)
        for b in range(F // QB):
            near = pl.ds(MEM + b * QB, 2 * QB)
            q = q4[b]
            s = jnp.concatenate([dot_nt(q, kk[pl.ds(0, MEM), :]), dot_nt(q, kk[near, :])], axis=1)
            s = (s.reshape(4, QB, KW) + bias[b][None]).reshape(4 * QB, KW)
            peak = jnp.max(s, axis=1, keepdims=True)
            w = jnp.exp2(s - peak)
            total = jnp.sum(w, axis=1, keepdims=True)
            w = w.astype(BF)
            o = dot_nn(w[:, :MEM], vv[pl.ds(0, MEM), :]) + dot_nn(w[:, MEM:], vv[near, :])
            o, total = o.reshape(4, QB, GW), total.reshape(4, QB, 1)
            out, den = o[3], jnp.broadcast_to(total[3], (QB, GW))
            for h in range(3):
                out = jnp.where(lane_head == h, o[h], out)
                den = jnp.where(lane_head == h, total[h], den)
            att[b * QB : (b + 1) * QB, columns] = (out / den).astype(BF)
        after_attention(j)

    out_end()

    for ch in range(NCH):
        features = slice(ch * CH, (ch + 1) * CH)
        w = owg[pl.ds(ch * (NX // NCH), NX // NCH)].reshape(CH, D)
        for b in range(2):
            rows = slice(b * 256, (b + 1) * 256)
            o = dot_nt(att[rows, :], w)
            live = first_frame + b * 256 + lax.broadcasted_iota(jnp.int32, (256, 1), 0) < length
            enc[rows, features] = jnp.where(
                live, frames[rows, features].astype(F32) + o, 0.0
            ).astype(BF)
        sent = dot_nn(ri[...], enc[:, features]) / cnt[:, :1]
        sb[ch] = sent.reshape(N_TM, CAP, CH).astype(BF)

        @pl.loop(1, N_TM)
        def _(d):
            to = lax.rem(t + d, N_TM)
            remote(sb.at[ch, to], rb.at[ch, t], a_send.at[ch, d], a_recv.at[ch, d], (r, to)).start()

        rb[ch, t] = sb[ch, t]

    enc_out = pltpu.make_async_copy(enc, enc_hbm, out_sem.at[0])
    enc_out.start()
    lw_step_three()

    def sent_core(v):
        for e in (1, 2, 3):
            if e != 2:
                ref = w_group(v, 0)
                remote(ref, ref, xw_send.at[e], xw_recv.at[e], sib).wait_send()
            ref = mg.at[x] if v == 0 else mg.at[x, z]
            remote(ref, ref, xm_send.at[e], xm_recv.at[e], sib).wait_send()
        for e in (0, 1, 3):
            to_sibling(v, e).wait_send()

    per_core(sent_core)
    remote(far_z(z), far_z(z), x2_send.at[0], x2_recv.at[0], sib).wait_send()
    for d in range(1, NZ):
        remote(far_z(z), far_z(z), z2_send.at[d], z2_recv.at[d], sib).wait_send()
    for by in range(NY):
        ref = far_piece(wrap(y - by, NY) * 2 + c)
        remote(ref, ref, s2_send.at[by], s2_recv.at[by], sib).wait_send()
        if by:
            remote(ref, ref, y2_send.at[by], y2_recv.at[by], sib).wait_send()
    for d in range(1, NZ):
        remote(o_z(z), o_z(z), oz_send.at[d], oz_recv.at[d], sib).wait_send()
    for e in (1, 2, 3):
        remote(o_x(0), o_x(0), ox_send.at[e], ox_recv.at[e], sib).wait_send()
        remote(o_y(0, c), o_y(0, c), oy_send.at[e], oy_recv.at[e], sib).wait_send()
    for by in range(NY):
        ref = o_y(by, c)
        remote(ref, ref, os_send.at[by], os_recv.at[by], sib).wait_send()
    for k, slot in enumerate((r, lw_down, lw_up, lw_far)):
        side(lwg.at[slot], k).wait_send()
        side(lwg.at[slot + 1 - 2 * c], k).wait_recv()
    hop(lwg.at[r], 0).wait_send()
    hop(lwg.at[r], 1).wait_send()
    hop(lw_half(r, 0), 2).wait_send()
    hop(lw_half(r, 0), 3).wait_send()

    def lm_out(k):
        return pltpu.make_async_copy(
            lmo.at[k], lm_hbm.at[:, pl.ds(k * 256, 256)], out_sem.at[1 + k]
        )

    for ch in range(NCH):

        @pl.loop(1, N_TM)
        def _(d):
            to = lax.rem(t + d, N_TM)
            source = wrap(t - d, N_TM)
            copy = remote(
                sb.at[ch, to], rb.at[ch, source], a_send.at[ch, d], a_recv.at[ch, d], (r, to)
            )
            copy.wait_recv()
            copy.wait_send()

        got = rb[ch].astype(F32).reshape(SLOTS, CH).astype(BF)
        for k in range(2 * NY):
            part = dot_nn(got, lwg[k, ch * CH : (ch + 1) * CH, :])
            if ch > 0:
                part += lacc[k]
            if ch < NCH - 1:
                lacc[k] = part
            else:
                lmo[k] = part.astype(BF)
                lm_out(k).start()
    enc_out.wait()
    for k in range(2 * NY):
        lm_out(k).wait()


def per_device(
    frames, lengths, norm_gain, memory_gain, qkv_weight, out_weight, segment_ids, owners, language_weight
):
    vmem = pl.BlockSpec(memory_space=pltpu.VMEM)
    smem = pl.BlockSpec(memory_space=pltpu.SMEM)
    hbm = pl.BlockSpec(memory_space=pl.ANY)
    dma = pltpu.SemaphoreType.DMA
    enc, lm = pl.pallas_call(
        kernel,
        out_shape=(
            jax.ShapeDtypeStruct((F, D), BF),
            jax.ShapeDtypeStruct((SLOTS, DL), BF),
        ),
        in_specs=[vmem, smem, vmem, vmem, hbm, hbm, vmem, vmem, hbm],
        out_specs=(hbm, hbm),
        scratch_shapes=[
            pltpu.VMEM((3, NX, NZ, 2, 16, D), BF),
            pltpu.VMEM((NX, NZ, 32, D), BF),
            pltpu.VMEM((2 * NY, D, DL // (2 * NY)), BF),
            pltpu.VMEM((F + 16, D), BF),
            pltpu.VMEM((NX, NZ, 16, D), BF),
            pltpu.VMEM((F // C, D), F32),
            pltpu.VMEM((F // QB, 4 * QB, GW), BF),
            pltpu.VMEM((MEM + F + QB, GW), BF),
            pltpu.VMEM((MEM + F + QB, GW), BF),
            pltpu.VMEM((F, D), BF),
            pltpu.VMEM((F // QB, QB, KW), F32),
            pltpu.VMEM((SLOTS, F), BF),
            pltpu.VMEM((SLOTS, 128), F32),
            pltpu.VMEM((F, D), BF),
            pltpu.VMEM((NCH, N_TM, CAP, CH), BF),
            pltpu.VMEM((NCH, N_TM, CAP, CH), BF),
            pltpu.VMEM((2 * NY, SLOTS, 256), F32),
            pltpu.VMEM((2 * NY, SLOTS, DL // (2 * NY)), BF),
            dma((8,)), dma((8,)), dma((8,)), dma((8,)), dma((4,)), dma((4,)), dma((4,)), dma((4,)),
            dma((4,)), dma((4,)),
            dma((1,)), dma((1,)), dma((8,)), dma((8,)), dma((4,)), dma((4,)), dma((4,)), dma((4,)),
            dma((8,)), dma((8,)), dma((4,)), dma((4,)), dma((4,)), dma((4,)), dma((4,)), dma((4,)),
            dma((1,)), dma((1,)), dma((4,)), dma((4,)), dma((4,)), dma((4,)),
            dma((NCH, N_TM)), dma((NCH, N_TM)), dma((3,)), dma((1 + 2 * NY,)),
        ],
        compiler_params=pltpu.CompilerParams(
            collective_id=0, has_side_effects=True, vmem_limit_bytes=58 * 2**20
        ),
        name="block",
    )(
        frames[0],
        lengths,
        norm_gain[None],
        memory_gain[None],
        qkv_weight.transpose(0, 2, 1).reshape(3, 2, 16, D),
        out_weight.T,
        segment_ids[0],
        owners[0, :, :, 0],
        language_weight,
    )
    return (enc[None], lm[None, None])


def solution(mesh):
    in_specs = (
        P("rec", "tm", None),
        P("rec"),
        P(),
        P(),
        P(None, None, "tm"),
        P(None, "tm"),
        P("rec", "tm", None),
        P("rec", "tm", None, None),
        P(None, "rec"),
    )
    out_specs = (P("rec", "tm", None), P("rec", "tm", None, None))
    return jax.shard_map(
        per_device, mesh=mesh, in_specs=in_specs, out_specs=out_specs, check_vma=False
    )
```

```python
import functools

import jax
import jax.numpy as jnp
from jax import lax
from jax.experimental import pallas as pl
from jax.experimental.pallas import tpu as pltpu
from jax.sharding import PartitionSpec as P

H = 16
C = 32
RC = 8
EPS_NORM = 1e-05
EPS_MEMORY = 1e-06
NEG_BIG = -1e30

NX, NZ, NY = 4, 8, 4
N_TM = NX * NZ
F = 512
D = 1024
DL = 2048
TOK = 128
CAP = 8
SLOTS = 256
G = 4
GW = D // G
HEAD = D // H
QB = 64
MEM = N_TM * F // C
KW = MEM + 2 * QB
NCH = 2
CH = D // NCH
LOG2E = 1.4426950408889634
BF = jnp.bfloat16
F32 = jnp.float32


def dot_nt(a, b):
    return lax.dot_general(a, b, (((1,), (1,)), ((), ())), preferred_element_type=F32)


def dot_nn(a, b):
    return lax.dot_general(a, b, (((1,), (0,)), ((), ())), preferred_element_type=F32)


def wrap(a, n):
    return lax.rem(a + 2 * n, n)


def kernel(
    frames, lengths, norm_gain, memory_gain, wq_hbm, wo_hbm, segments, owners, lw_hbm,
    enc_hbm, lm_hbm,
    wg, owg, lwg, xs, mg, mrows, q4, kk, vv, att, bias, ri, cnt, enc, sb, rb, lacc, lmo,
    zw_send, zw_recv, zm_send, zm_recv, xw_send, xw_recv, xm_send, xm_recv, sw_send, sw_recv,
    x2_send, x2_recv, z2_send, z2_recv, y2_send, y2_recv, s2_send, s2_recv,
    oz_send, oz_recv, ox_send, ox_recv, oy_send, oy_recv, os_send, os_recv,
    r_send, r_recv, l_send, l_recv, ls_send, ls_recv, a_send, a_recv, own_sem, out_sem,
):
    r = lax.axis_index("rec")
    t = lax.axis_index("tm")
    y, c = r // 2, lax.rem(r, 2)
    x, z = t // NZ, lax.rem(t, NZ)
    sib = (y * 2 + (1 - c), t)
    first_frame = t * F
    length = lengths[0]

    barrier = pltpu.get_barrier_semaphore()

    @pl.loop(1, N_TM)
    def _(d):
        pl.semaphore_signal(
            barrier, inc=1, device_id=(r, lax.rem(t + d, N_TM)), device_id_type=pl.DeviceIdType.MESH
        )

    @pl.loop(1, 2 * NY)
    def _(d):
        pl.semaphore_signal(
            barrier, inc=1, device_id=(lax.rem(r + d, 2 * NY), t), device_id_type=pl.DeviceIdType.MESH
        )

    span0 = t * (F // C)

    @pl.loop(0, F // QB)
    def _(b):
        q = b * QB + lax.broadcasted_iota(jnp.int32, (QB, KW), 0)
        n = lax.broadcasted_iota(jnp.int32, (QB, KW), 1)
        q_span = q // C
        u = b * QB + n - MEM
        in_memory = (n < MEM) & (n < span0 + q_span) & (n * C < length)
        same = (u // C) == q_span
        ahead = (u >= (q_span + 1) * C) & (u < (q_span + 1) * C + RC)
        in_frames = (n >= MEM) & (same | ahead) & (first_frame + u < length)
        bias[b] = jnp.where(in_memory | in_frames, 0.0, NEG_BIG)

    own_row = jnp.broadcast_to(owners[...].astype(F32), (TOK, TOK))
    own_col = own_row.T
    earlier = lax.broadcasted_iota(jnp.int32, (TOK, TOK), 0) < lax.broadcasted_iota(
        jnp.int32, (TOK, TOK), 1
    )
    slot = jnp.sum(jnp.where((own_row == own_col) & earlier, 1.0, 0.0), axis=0, keepdims=True)
    target = owners[...].astype(F32) * CAP + slot
    place = lax.broadcasted_iota(jnp.int32, (SLOTS, TOK), 0).astype(F32)
    route = jnp.where(place == target, 1.0, 0.0).astype(BF)
    member = jnp.where(
        lax.broadcasted_iota(jnp.int32, (TOK, F), 0) == segments[...], 1.0, 0.0
    ).astype(BF)
    chosen = dot_nn(route, member)
    ri[...] = chosen.astype(BF)
    cnt[...] = jnp.broadcast_to(
        jnp.maximum(jnp.sum(chosen, axis=1, keepdims=True), 1.0), (SLOTS, 128)
    )
    kk[pl.ds(MEM + F, QB), :] = jnp.zeros((QB, GW), BF)
    vv[pl.ds(MEM + F, QB), :] = jnp.zeros((QB, GW), BF)

    pl.semaphore_wait(barrier, N_TM - 1 + 2 * NY - 1)

    def remote(src, dst, send, recv, device):
        return pltpu.make_async_remote_copy(
            src_ref=src,
            dst_ref=dst,
            send_sem=send,
            recv_sem=recv,
            device_id=device,
            device_id_type=pl.DeviceIdType.MESH,
        )

    def at_z(by):
        return (r, x * NZ + wrap(z + by, NZ))

    def at_x(by):
        return (r, wrap(x + by, NX) * NZ + z)

    def at_y(by):
        return (wrap(y + by, NY) * 2 + c, t)

    def per_core(fn):
        for v in (0, 1):
            pl.when(c == v)(functools.partial(fn, v))

    ZK = NZ // 2

    def halved(ref, k, d):
        if k < ZK:
            return ref
        return ref.at[(slice(None),) * (len(ref.shape) - 1) + (pl.ds(d * (D // 2), D // 2),)]

    def ring_start(k, piece, send, recv, own=None):
        for d, s in enumerate((1, -1)):
            dst = halved(piece(wrap(z - s * (k - 1), NZ)), k, d)
            n = 2 * (k - 1) + d
            remote(own if own is not None else dst, dst, send.at[n], recv.at[n], at_z(s)).start()

    def ring_wait(k, piece, send, recv):
        for d, s in enumerate((1, -1)):
            ref = halved(piece(wrap(z - s * k, NZ)), k, d)
            n = 2 * (k - 1) + d
            copy = remote(ref, ref, send.at[n], recv.at[n], at_z(s))
            copy.wait_recv()
            copy.wait_send()

    def arrived(k):
        return [wrap(z - k, NZ)] + ([wrap(z + k, NZ)] if k < ZK else [])

    def group(e):
        return wrap(x - e, NX)

    def w_ring(v, e):
        return lambda o: wg.at[:, group(e), o, v]

    def w_group(v, e):
        return wg.at[:, group(e), :, v]

    def m_ring(v):
        return (lambda o: mg.at[x, o]) if v == 0 else (lambda o: mg.at[:, o])

    def across_start(src, dst, send, recv, peers):
        for e in peers:
            remote(src, dst, send.at[e], recv.at[e], at_x(e)).start()

    def w_across(v, e):
        return w_group(v, e)

    def m_across(v, e):
        return mg.at[group(e)] if v == 0 else mg.at[group(e), z]

    def across_wait(ref, recv, e):
        remote(ref, ref, xw_send.at[e], recv.at[e], at_x(e)).wait_recv()

    def to_sibling(v, e):
        return remote(w_group(v, e), w_group(v, e), sw_send.at[e], sw_recv.at[e], sib)

    def from_sibling(e):
        def wait(v):
            to_sibling(1 - v, e).wait_recv()

        per_core(wait)

    lanes = pl.ds(pl.multiple_of(r * 128, 128), 128)

    def first_hop(v):
        own = wq_hbm.at[:, v]
        ring_start(1, w_ring(v, 0), zw_send, zw_recv, own=own)
        across_start(own, wg.at[:, x, z, v], xw_send, xw_recv, (1, 3))

    per_core(first_hop)
    far_first = remote(
        wq_hbm.at[:, :, :, lanes], wg.at[:, x, z, :, :, lanes], x2_send.at[0], x2_recv.at[0], at_x(2)
    )
    far_first.start()
    for d in range(1, NZ):
        remote(
            wo_hbm.at[:, lanes], owg.at[x, z, :, lanes], oz_send.at[d], oz_recv.at[d], at_z(d)
        ).start()
    own_copies = [
        pltpu.make_async_copy(
            wq_hbm.at[:, c], wg.at[:, x, z, c], own_sem.at[0]
        ),
        pltpu.make_async_copy(wo_hbm.at[:, lanes], owg.at[x, z, :, lanes], own_sem.at[1]),
        pltpu.make_async_copy(lw_hbm, lwg.at[r], own_sem.at[2]),
    ]
    for copy in own_copies:
        copy.start()

    gain = norm_gain[...]

    @pl.loop(0, F // C)
    def _(i):
        rows = pl.ds(pl.multiple_of(i * C, C), C)
        v = frames[rows, :].astype(F32)
        centred = v - jnp.mean(v, axis=1, keepdims=True)
        spread = jnp.mean(centred * centred, axis=1, keepdims=True)
        normed = (centred * lax.rsqrt(spread + EPS_NORM) * gain).astype(BF)
        xs[rows, :] = normed
        start = first_frame + i * C
        live = start + lax.broadcasted_iota(jnp.int32, (C, 1), 0) < length
        total = jnp.sum(jnp.where(live, normed.astype(F32), 0.0), axis=0, keepdims=True)
        count = jnp.clip(length - start, 1, C).astype(F32)
        mrows[pl.ds(i, 1), :] = total / count

    means = mrows[...]
    power = jnp.mean(means * means, axis=1, keepdims=True)
    mg[x, z] = (means * lax.rsqrt(power + EPS_MEMORY) * memory_gain[...]).astype(BF)

    def round_one(v):
        ring_next(v, 1)
        across_start(mg.at[x, z], mg.at[x, z], xm_send, xm_recv, (1, 3, 2))
        if v == 0:
            ring_start(1, m_ring(v), zm_send, zm_recv)

    def ring_next(v, k):
        ring_wait(k, w_ring(v, 0), zw_send, zw_recv)
        if k < ZK:
            ring_start(k + 1, w_ring(v, 0), zw_send, zw_recv)
        else:
            to_sibling(v, 0).start()
        for o in arrived(k):
            across_start(w_ring(v, 0)(o), w_ring(v, 0)(o), xw_send, xw_recv, (1, 3))

    def memory_next(v, k):
        ring_wait(k, m_ring(v), zm_send, zm_recv)
        if k < ZK:
            ring_start(k + 1, m_ring(v), zm_send, zm_recv)
        if v == 0:
            for o in arrived(k):
                across_start(mg.at[x, o], mg.at[x, o], xm_send, xm_recv, (1, 3, 2))

    for copy in own_copies:
        copy.wait()
    per_core(round_one)

    right = remote(
        xs.at[pl.ds(0, 16)], xs.at[pl.ds(F, 16)], r_send.at[0], r_recv.at[0], (r, wrap(t - 1, N_TM))
    )
    right.start()

    def o_z(o):
        return owg.at[x, o, :, lanes]

    def o_x(e):
        return owg.at[group(e), :, :, lanes]

    def o_y(by, core):
        return owg.at[:, :, :, pl.ds(pl.multiple_of((wrap(y - by, NY) * 2 + core) * 128, 128), 128)]

    def out_across():
        for d in range(1, NZ):
            ref = o_z(wrap(z - d, NZ))
            remote(ref, ref, oz_send.at[d], oz_recv.at[d], at_z(d)).wait_recv()
        for e in (1, 3, 2):
            remote(o_x(0), o_x(0), ox_send.at[e], ox_recv.at[e], at_x(e)).start()

    def out_up():
        for e in (1, 3, 2):
            remote(o_x(e), o_x(e), ox_send.at[e], ox_recv.at[e], at_x(e)).wait_recv()
        for by in (1, 3, 2):
            remote(o_y(0, c), o_y(0, c), oy_send.at[by], oy_recv.at[by], at_y(by)).start()
        remote(o_y(0, c), o_y(0, c), os_send.at[0], os_recv.at[0], sib).start()

    def out_side():
        for by in (1, 3, 2):
            ref = o_y(by, c)
            remote(ref, ref, oy_send.at[by], oy_recv.at[by], at_y(by)).wait_recv()
            remote(ref, ref, os_send.at[by], os_recv.at[by], sib).start()

    def out_end():
        for by in range(NY):
            ref = o_y(by, 1 - c)
            remote(ref, ref, os_send.at[by], os_recv.at[by], sib).wait_recv()

    out_across()

    lw_up, lw_down, lw_far = (wrap(y + k, NY) * 2 + c for k in (1, -1, 2))

    def lw_half(slot, d):
        return lwg.at[slot, pl.ds(d * (D // 2), D // 2)]

    def hop(ref, k, device=sib):
        return remote(ref, ref, l_send.at[k], l_recv.at[k], device)

    def side(ref, k):
        return remote(ref, ref, ls_send.at[k], ls_recv.at[k], sib)

    hop(lwg.at[r], 0, at_y(1)).start()
    hop(lwg.at[r], 1, at_y(-1)).start()
    side(lwg.at[r], 0).start()

    def lw_step_two():
        hop(lwg.at[lw_down], 0).wait_recv()
        hop(lwg.at[lw_up], 1).wait_recv()
        hop(lw_half(lw_down, 0), 2, at_y(1)).start()
        hop(lw_half(lw_up, 1), 3, at_y(-1)).start()
        side(lwg.at[lw_down], 1).start()
        side(lwg.at[lw_up], 2).start()

    def lw_step_three():
        hop(lw_half(lw_far, 0), 2).wait_recv()
        hop(lw_half(lw_far, 1), 3).wait_recv()
        side(lwg.at[lw_far], 3).start()

    def round_two(v):
        if v == 1:
            for e in (1, 3, 2):
                across_wait(m_across(1, e), xm_recv, e)
            ring_start(1, m_ring(v), zm_send, zm_recv)
        else:
            memory_next(v, 1)
        ring_next(v, 2)

    def round_three(v):
        if v == 1:
            memory_next(v, 1)
            ring_next(v, 3)
        else:
            ring_next(v, 3)
            memory_next(v, 2)

    def round_four(v):
        if v == 1:
            memory_next(v, 2)
            ring_next(v, 4)
        else:
            ring_next(v, 4)
            memory_next(v, 3)

    def round_five(v):
        memory_next(v, 3 if v == 1 else 4)

    def round_six(v):
        if v == 1:
            memory_next(v, 4)
        else:
            for e in (1, 3, 2):
                across_wait(m_across(0, e), xm_recv, e)

    def x_next(e):
        def one(v):
            across_wait(w_across(v, e), xw_recv, e)
            to_sibling(v, e).start()

        per_core(one)

    def far_piece(rec):
        return wg.at[:, group(2), :, :, :, pl.ds(pl.multiple_of(rec * 128, 128), 128)]

    def far_z(o):
        return wg.at[:, group(2), o, :, :, lanes]

    def far_along():
        remote(far_z(z), far_z(z), x2_send.at[0], x2_recv.at[0], at_x(2)).wait_recv()
        for d in (4, 3, 5, 2, 6, 1, 7):
            remote(far_z(z), far_z(z), z2_send.at[d], z2_recv.at[d], at_z(d)).start()

    def far_up():
        for d in range(1, NZ):
            ref = far_z(wrap(z - d, NZ))
            remote(ref, ref, z2_send.at[d], z2_recv.at[d], at_z(d)).wait_recv()
        ref = far_piece(r)
        for by in (1, 3, 2):
            remote(ref, ref, y2_send.at[by], y2_recv.at[by], at_y(by)).start()
        remote(ref, ref, s2_send.at[0], s2_recv.at[0], sib).start()

    def far_side():
        for by in (1, 3, 2):
            ref = far_piece(wrap(y - by, NY) * 2 + c)
            remote(ref, ref, y2_send.at[by], y2_recv.at[by], at_y(by)).wait_recv()
            remote(ref, ref, s2_send.at[by], s2_recv.at[by], sib).start()

    def far_end():
        for by in range(NY):
            ref = far_piece(wrap(y - by, NY) * 2 + 1 - c)
            remote(ref, ref, s2_send.at[by], s2_recv.at[by], sib).wait_recv()

    per_core(round_two)
    per_core(round_three)
    per_core(round_four)
    out_up()
    far_along()
    per_core(round_five)
    from_sibling(0)
    right.wait()
    lane_head = lax.broadcasted_iota(jnp.int32, (1, GW), 1) // HEAD

    def project_frames(g):
        a = xs[...]
        q = dot_nt(a, wg[0, g].reshape(GW, D))[:F] * (HEAD**-0.5 * LOG2E)
        for h in range(4):
            q4[:, h * QB : (h + 1) * QB, :] = (
                jnp.where(lane_head == h, q, 0.0).astype(BF).reshape(F // QB, QB, GW)
            )
        for n, ref in ((1, kk), (2, vv)):
            ref[pl.ds(MEM, F + 16), :] = dot_nt(a, wg[n, g].reshape(GW, D)).astype(BF)

    project_frames(x)
    per_core(round_six)

    def before_projection(j):
        @pl.when(j == 1)
        def _():
            from_sibling(1)

        @pl.when(j == 2)
        def _():
            from_sibling(3)

        @pl.when(j == 3)
        def _():
            far_end()

    def after_projection(j):
        @pl.when(j == 0)
        def _():
            x_next(1)
            far_up()

        @pl.when(j == 1)
        def _():
            out_side()

        @pl.when(j == 3)
        def _():
            lw_step_two()

    def after_attention(j):
        @pl.when(j == 0)
        def _():
            x_next(3)

        @pl.when(j == 2)
        def _():
            far_side()

    @pl.loop(0, G)
    def _(j):
        before_projection(j)
        g = wrap(x - (j + (j // 2) * (5 - 2 * j)), NX)

        @pl.when(j > 0)
        def _():
            project_frames(g)

        m = mg[...].reshape(MEM, D)
        for n, ref in ((1, kk), (2, vv)):
            ref[pl.ds(0, MEM), :] = dot_nt(m, wg[n, g].reshape(GW, D)).astype(BF)
        after_projection(j)
        columns = pl.ds(pl.multiple_of(g * GW, GW), GW)
        for b in range(F // QB):
            near = pl.ds(MEM + b * QB, 2 * QB)
            q = q4[b]
            s = jnp.concatenate([dot_nt(q, kk[pl.ds(0, MEM), :]), dot_nt(q, kk[near, :])], axis=1)
            s = (s.reshape(4, QB, KW) + bias[b][None]).reshape(4 * QB, KW)
            peak = jnp.max(s, axis=1, keepdims=True)
            w = jnp.exp2(s - peak)
            total = jnp.sum(w, axis=1, keepdims=True)
            w = w.astype(BF)
            o = dot_nn(w[:, :MEM], vv[pl.ds(0, MEM), :]) + dot_nn(w[:, MEM:], vv[near, :])
            o, total = o.reshape(4, QB, GW), total.reshape(4, QB, 1)
            out, den = o[3], jnp.broadcast_to(total[3], (QB, GW))
            for h in range(3):
                out = jnp.where(lane_head == h, o[h], out)
                den = jnp.where(lane_head == h, total[h], den)
            att[b * QB : (b + 1) * QB, columns] = (out / den).astype(BF)
        after_attention(j)

    out_end()

    for ch in range(NCH):
        features = slice(ch * CH, (ch + 1) * CH)
        w = owg[pl.ds(ch * (NX // NCH), NX // NCH)].reshape(CH, D)
        for b in range(2):
            rows = slice(b * 256, (b + 1) * 256)
            o = dot_nt(att[rows, :], w)
            live = first_frame + b * 256 + lax.broadcasted_iota(jnp.int32, (256, 1), 0) < length
            enc[rows, features] = jnp.where(
                live, frames[rows, features].astype(F32) + o, 0.0
            ).astype(BF)
        sent = dot_nn(ri[...], enc[:, features]) / cnt[:, :1]
        sb[ch] = sent.reshape(N_TM, CAP, CH).astype(BF)

        @pl.loop(1, N_TM)
        def _(d):
            to = lax.rem(t + d, N_TM)
            remote(sb.at[ch, to], rb.at[ch, t], a_send.at[ch, d], a_recv.at[ch, d], (r, to)).start()

        rb[ch, t] = sb[ch, t]

    enc_out = pltpu.make_async_copy(enc, enc_hbm, out_sem.at[0])
    enc_out.start()
    lw_step_three()

    def sent_core(v):
        for e in (1, 2, 3):
            if e != 2:
                ref = w_group(v, 0)
                remote(ref, ref, xw_send.at[e], xw_recv.at[e], sib).wait_send()
            ref = mg.at[x] if v == 0 else mg.at[x, z]
            remote(ref, ref, xm_send.at[e], xm_recv.at[e], sib).wait_send()
        for e in (0, 1, 3):
            to_sibling(v, e).wait_send()

    per_core(sent_core)
    remote(far_z(z), far_z(z), x2_send.at[0], x2_recv.at[0], sib).wait_send()
    for d in range(1, NZ):
        remote(far_z(z), far_z(z), z2_send.at[d], z2_recv.at[d], sib).wait_send()
    for by in range(NY):
        ref = far_piece(wrap(y - by, NY) * 2 + c)
        remote(ref, ref, s2_send.at[by], s2_recv.at[by], sib).wait_send()
        if by:
            remote(ref, ref, y2_send.at[by], y2_recv.at[by], sib).wait_send()
    for d in range(1, NZ):
        remote(o_z(z), o_z(z), oz_send.at[d], oz_recv.at[d], sib).wait_send()
    for e in (1, 2, 3):
        remote(o_x(0), o_x(0), ox_send.at[e], ox_recv.at[e], sib).wait_send()
        remote(o_y(0, c), o_y(0, c), oy_send.at[e], oy_recv.at[e], sib).wait_send()
    for by in range(NY):
        ref = o_y(by, c)
        remote(ref, ref, os_send.at[by], os_recv.at[by], sib).wait_send()
    for k, slot in enumerate((r, lw_down, lw_up, lw_far)):
        side(lwg.at[slot], k).wait_send()
        side(lwg.at[slot + 1 - 2 * c], k).wait_recv()
    hop(lwg.at[r], 0).wait_send()
    hop(lwg.at[r], 1).wait_send()
    hop(lw_half(r, 0), 2).wait_send()
    hop(lw_half(r, 0), 3).wait_send()

    def lm_out(k):
        return pltpu.make_async_copy(
            lmo.at[k], lm_hbm.at[:, pl.ds(k * 256, 256)], out_sem.at[1 + k]
        )

    for ch in range(NCH):

        @pl.loop(1, N_TM)
        def _(d):
            to = lax.rem(t + d, N_TM)
            source = wrap(t - d, N_TM)
            copy = remote(
                sb.at[ch, to], rb.at[ch, source], a_send.at[ch, d], a_recv.at[ch, d], (r, to)
            )
            copy.wait_recv()
            copy.wait_send()

        got = rb[ch].astype(F32).reshape(SLOTS, CH).astype(BF)
        for k in range(2 * NY):
            part = dot_nn(got, lwg[k, ch * CH : (ch + 1) * CH, :])
            if ch > 0:
                part += lacc[k]
            if ch < NCH - 1:
                lacc[k] = part
            else:
                lmo[k] = part.astype(BF)
                lm_out(k).start()
    enc_out.wait()
    for k in range(2 * NY):
        lm_out(k).wait()


def per_device(
    frames, lengths, norm_gain, memory_gain, qkv_weight, out_weight, segment_ids, owners, language_weight
):
    vmem = pl.BlockSpec(memory_space=pltpu.VMEM)
    smem = pl.BlockSpec(memory_space=pltpu.SMEM)
    hbm = pl.BlockSpec(memory_space=pl.ANY)
    dma = pltpu.SemaphoreType.DMA
    enc, lm = pl.pallas_call(
        kernel,
        out_shape=(
            jax.ShapeDtypeStruct((F, D), BF),
            jax.ShapeDtypeStruct((SLOTS, DL), BF),
        ),
        in_specs=[vmem, smem, vmem, vmem, hbm, hbm, vmem, vmem, hbm],
        out_specs=(hbm, hbm),
        scratch_shapes=[
            pltpu.VMEM((3, NX, NZ, 2, 16, D), BF),
            pltpu.VMEM((NX, NZ, 32, D), BF),
            pltpu.VMEM((2 * NY, D, DL // (2 * NY)), BF),
            pltpu.VMEM((F + 16, D), BF),
            pltpu.VMEM((NX, NZ, 16, D), BF),
            pltpu.VMEM((F // C, D), F32),
            pltpu.VMEM((F // QB, 4 * QB, GW), BF),
            pltpu.VMEM((MEM + F + QB, GW), BF),
            pltpu.VMEM((MEM + F + QB, GW), BF),
            pltpu.VMEM((F, D), BF),
            pltpu.VMEM((F // QB, QB, KW), F32),
            pltpu.VMEM((SLOTS, F), BF),
            pltpu.VMEM((SLOTS, 128), F32),
            pltpu.VMEM((F, D), BF),
            pltpu.VMEM((NCH, N_TM, CAP, CH), BF),
            pltpu.VMEM((NCH, N_TM, CAP, CH), BF),
            pltpu.VMEM((2 * NY, SLOTS, 256), F32),
            pltpu.VMEM((2 * NY, SLOTS, DL // (2 * NY)), BF),
            dma((8,)), dma((8,)), dma((8,)), dma((8,)), dma((4,)), dma((4,)), dma((4,)), dma((4,)),
            dma((4,)), dma((4,)),
            dma((1,)), dma((1,)), dma((8,)), dma((8,)), dma((4,)), dma((4,)), dma((4,)), dma((4,)),
            dma((8,)), dma((8,)), dma((4,)), dma((4,)), dma((4,)), dma((4,)), dma((4,)), dma((4,)),
            dma((1,)), dma((1,)), dma((4,)), dma((4,)), dma((4,)), dma((4,)),
            dma((NCH, N_TM)), dma((NCH, N_TM)), dma((3,)), dma((1 + 2 * NY,)),
        ],
        compiler_params=pltpu.CompilerParams(
            collective_id=0, has_side_effects=True, vmem_limit_bytes=58 * 2**20
        ),
        name="block",
    )(
        frames[0],
        lengths,
        norm_gain[None],
        memory_gain[None],
        qkv_weight.transpose(0, 2, 1).reshape(3, 2, 16, D),
        out_weight.T,
        segment_ids[0],
        owners[0, :, :, 0],
        language_weight,
    )
    return (enc[None], lm[None, None])


def solution(mesh):
    in_specs = (
        P("rec", "tm", None),
        P("rec"),
        P(),
        P(),
        P(None, None, "tm"),
        P(None, "tm"),
        P("rec", "tm", None),
        P("rec", "tm", None, None),
        P(None, "rec"),
    )
    out_specs = (P("rec", "tm", None), P("rec", "tm", None, None))
    return jax.shard_map(
        per_device, mesh=mesh, in_specs=in_specs, out_specs=out_specs, check_vma=False
    )
```

```python
import functools

import jax
import jax.numpy as jnp
from jax import lax
from jax.experimental import pallas as pl
from jax.experimental.pallas import tpu as pltpu
from jax.sharding import PartitionSpec as P

H = 16
C = 32
RC = 8
EPS_NORM = 1e-05
EPS_MEMORY = 1e-06
NEG_BIG = -1e30

NX, NZ, NY = 4, 8, 4
N_TM = NX * NZ
F = 512
D = 1024
DL = 2048
TOK = 128
CAP = 8
SLOTS = 256
G = 4
GW = D // G
HEAD = D // H
QB = 64
MEM = N_TM * F // C
KW = MEM + 2 * QB
NCH = 1
CH = D // NCH
LOG2E = 1.4426950408889634
BF = jnp.bfloat16
F32 = jnp.float32


def dot_nt(a, b):
    return lax.dot_general(a, b, (((1,), (1,)), ((), ())), preferred_element_type=F32)


def dot_nn(a, b):
    return lax.dot_general(a, b, (((1,), (0,)), ((), ())), preferred_element_type=F32)


def wrap(a, n):
    return lax.rem(a + 2 * n, n)


def kernel(
    frames, lengths, norm_gain, memory_gain, wq_hbm, wo_hbm, segments, owners, lw_hbm,
    enc_hbm, lm_hbm,
    wg, owg, lwg, xs, mg, mrows, q4, kk, vv, att, bias, ri, cnt, enc, sb, rb, lacc, lmo,
    zw_send, zw_recv, zm_send, zm_recv, xw_send, xw_recv, xm_send, xm_recv, sw_send, sw_recv,
    x2_send, x2_recv, z2_send, z2_recv, y2_send, y2_recv, s2_send, s2_recv,
    oz_send, oz_recv, ox_send, ox_recv, oy_send, oy_recv, os_send, os_recv,
    r_send, r_recv, l_send, l_recv, ls_send, ls_recv, a_send, a_recv, own_sem, out_sem,
):
    r = lax.axis_index("rec")
    t = lax.axis_index("tm")
    y, c = r // 2, lax.rem(r, 2)
    x, z = t // NZ, lax.rem(t, NZ)
    sib = (y * 2 + (1 - c), t)
    first_frame = t * F
    length = lengths[0]

    barrier = pltpu.get_barrier_semaphore()

    @pl.loop(1, N_TM)
    def _(d):
        pl.semaphore_signal(
            barrier, inc=1, device_id=(r, lax.rem(t + d, N_TM)), device_id_type=pl.DeviceIdType.MESH
        )

    @pl.loop(1, 2 * NY)
    def _(d):
        pl.semaphore_signal(
            barrier, inc=1, device_id=(lax.rem(r + d, 2 * NY), t), device_id_type=pl.DeviceIdType.MESH
        )

    span0 = t * (F // C)

    @pl.loop(0, F // QB)
    def _(b):
        q = b * QB + lax.broadcasted_iota(jnp.int32, (QB, KW), 0)
        n = lax.broadcasted_iota(jnp.int32, (QB, KW), 1)
        q_span = q // C
        u = b * QB + n - MEM
        in_memory = (n < MEM) & (n < span0 + q_span) & (n * C < length)
        same = (u // C) == q_span
        ahead = (u >= (q_span + 1) * C) & (u < (q_span + 1) * C + RC)
        in_frames = (n >= MEM) & (same | ahead) & (first_frame + u < length)
        bias[b] = jnp.where(in_memory | in_frames, 0.0, NEG_BIG)

    own_row = jnp.broadcast_to(owners[...].astype(F32), (TOK, TOK))
    own_col = own_row.T
    earlier = lax.broadcasted_iota(jnp.int32, (TOK, TOK), 0) < lax.broadcasted_iota(
        jnp.int32, (TOK, TOK), 1
    )
    slot = jnp.sum(jnp.where((own_row == own_col) & earlier, 1.0, 0.0), axis=0, keepdims=True)
    target = owners[...].astype(F32) * CAP + slot
    place = lax.broadcasted_iota(jnp.int32, (SLOTS, TOK), 0).astype(F32)
    route = jnp.where(place == target, 1.0, 0.0).astype(BF)
    member = jnp.where(
        lax.broadcasted_iota(jnp.int32, (TOK, F), 0) == segments[...], 1.0, 0.0
    ).astype(BF)
    chosen = dot_nn(route, member)
    ri[...] = chosen.astype(BF)
    cnt[...] = jnp.broadcast_to(
        jnp.maximum(jnp.sum(chosen, axis=1, keepdims=True), 1.0), (SLOTS, 128)
    )
    kk[pl.ds(MEM + F, QB), :] = jnp.zeros((QB, GW), BF)
    vv[pl.ds(MEM + F, QB), :] = jnp.zeros((QB, GW), BF)

    pl.semaphore_wait(barrier, N_TM - 1 + 2 * NY - 1)

    def remote(src, dst, send, recv, device):
        return pltpu.make_async_remote_copy(
            src_ref=src,
            dst_ref=dst,
            send_sem=send,
            recv_sem=recv,
            device_id=device,
            device_id_type=pl.DeviceIdType.MESH,
        )

    def at_z(by):
        return (r, x * NZ + wrap(z + by, NZ))

    def at_x(by):
        return (r, wrap(x + by, NX) * NZ + z)

    def at_y(by):
        return (wrap(y + by, NY) * 2 + c, t)

    def per_core(fn):
        for v in (0, 1):
            pl.when(c == v)(functools.partial(fn, v))

    ZK = NZ // 2

    def halved(ref, k, d):
        if k < ZK:
            return ref
        return ref.at[(slice(None),) * (len(ref.shape) - 1) + (pl.ds(d * (D // 2), D // 2),)]

    def ring_start(k, piece, send, recv, own=None):
        for d, s in enumerate((1, -1)):
            dst = halved(piece(wrap(z - s * (k - 1), NZ)), k, d)
            n = 2 * (k - 1) + d
            remote(own if own is not None else dst, dst, send.at[n], recv.at[n], at_z(s)).start()

    def ring_wait(k, piece, send, recv):
        for d, s in enumerate((1, -1)):
            ref = halved(piece(wrap(z - s * k, NZ)), k, d)
            n = 2 * (k - 1) + d
            copy = remote(ref, ref, send.at[n], recv.at[n], at_z(s))
            copy.wait_recv()
            copy.wait_send()

    def arrived(k):
        return [wrap(z - k, NZ)] + ([wrap(z + k, NZ)] if k < ZK else [])

    def group(e):
        return wrap(x - e, NX)

    def w_ring(v, e):
        return lambda o: wg.at[:, group(e), o, v]

    def w_group(v, e):
        return wg.at[:, group(e), :, v]

    def m_ring(v):
        return (lambda o: mg.at[x, o]) if v == 0 else (lambda o: mg.at[:, o])

    def across_start(src, dst, send, recv, peers):
        for e in peers:
            remote(src, dst, send.at[e], recv.at[e], at_x(e)).start()

    def w_across(v, e):
        return w_group(v, e)

    def m_across(v, e):
        return mg.at[group(e)] if v == 0 else mg.at[group(e), z]

    def across_wait(ref, recv, e):
        remote(ref, ref, xw_send.at[e], recv.at[e], at_x(e)).wait_recv()

    def to_sibling(v, e):
        return remote(w_group(v, e), w_group(v, e), sw_send.at[e], sw_recv.at[e], sib)

    def from_sibling(e):
        def wait(v):
            to_sibling(1 - v, e).wait_recv()

        per_core(wait)

    lanes = pl.ds(pl.multiple_of(r * 128, 128), 128)

    def first_hop(v):
        own = wq_hbm.at[:, v]
        ring_start(1, w_ring(v, 0), zw_send, zw_recv, own=own)
        across_start(own, wg.at[:, x, z, v], xw_send, xw_recv, (1, 3))

    per_core(first_hop)
    far_first = remote(
        wq_hbm.at[:, :, :, lanes], wg.at[:, x, z, :, :, lanes], x2_send.at[0], x2_recv.at[0], at_x(2)
    )
    far_first.start()
    for d in range(1, NZ):
        remote(
            wo_hbm.at[:, lanes], owg.at[x, z, :, lanes], oz_send.at[d], oz_recv.at[d], at_z(d)
        ).start()
    own_copies = [
        pltpu.make_async_copy(
            wq_hbm.at[:, c], wg.at[:, x, z, c], own_sem.at[0]
        ),
        pltpu.make_async_copy(wo_hbm.at[:, lanes], owg.at[x, z, :, lanes], own_sem.at[1]),
        pltpu.make_async_copy(lw_hbm, lwg.at[r], own_sem.at[2]),
    ]
    for copy in own_copies:
        copy.start()

    gain = norm_gain[...]

    @pl.loop(0, F // C)
    def _(i):
        rows = pl.ds(pl.multiple_of(i * C, C), C)
        v = frames[rows, :].astype(F32)
        centred = v - jnp.mean(v, axis=1, keepdims=True)
        spread = jnp.mean(centred * centred, axis=1, keepdims=True)
        normed = (centred * lax.rsqrt(spread + EPS_NORM) * gain).astype(BF)
        xs[rows, :] = normed
        start = first_frame + i * C
        live = start + lax.broadcasted_iota(jnp.int32, (C, 1), 0) < length
        total = jnp.sum(jnp.where(live, normed.astype(F32), 0.0), axis=0, keepdims=True)
        count = jnp.clip(length - start, 1, C).astype(F32)
        mrows[pl.ds(i, 1), :] = total / count

    means = mrows[...]
    power = jnp.mean(means * means, axis=1, keepdims=True)
    mg[x, z] = (means * lax.rsqrt(power + EPS_MEMORY) * memory_gain[...]).astype(BF)

    def round_one(v):
        ring_next(v, 1)
        across_start(mg.at[x, z], mg.at[x, z], xm_send, xm_recv, (1, 3, 2))
        if v == 0:
            ring_start(1, m_ring(v), zm_send, zm_recv)

    def ring_next(v, k):
        ring_wait(k, w_ring(v, 0), zw_send, zw_recv)
        if k < ZK:
            ring_start(k + 1, w_ring(v, 0), zw_send, zw_recv)
        else:
            to_sibling(v, 0).start()
        for o in arrived(k):
            across_start(w_ring(v, 0)(o), w_ring(v, 0)(o), xw_send, xw_recv, (1, 3))

    def memory_next(v, k):
        ring_wait(k, m_ring(v), zm_send, zm_recv)
        if k < ZK:
            ring_start(k + 1, m_ring(v), zm_send, zm_recv)
        if v == 0:
            for o in arrived(k):
                across_start(mg.at[x, o], mg.at[x, o], xm_send, xm_recv, (1, 3, 2))

    for copy in own_copies:
        copy.wait()
    per_core(round_one)

    right = remote(
        xs.at[pl.ds(0, 16)], xs.at[pl.ds(F, 16)], r_send.at[0], r_recv.at[0], (r, wrap(t - 1, N_TM))
    )
    right.start()

    def o_z(o):
        return owg.at[x, o, :, lanes]

    def o_x(e):
        return owg.at[group(e), :, :, lanes]

    def o_y(by, core):
        return owg.at[:, :, :, pl.ds(pl.multiple_of((wrap(y - by, NY) * 2 + core) * 128, 128), 128)]

    def out_across():
        for d in range(1, NZ):
            ref = o_z(wrap(z - d, NZ))
            remote(ref, ref, oz_send.at[d], oz_recv.at[d], at_z(d)).wait_recv()
        for e in (1, 3, 2):
            remote(o_x(0), o_x(0), ox_send.at[e], ox_recv.at[e], at_x(e)).start()

    def out_up():
        for e in (1, 3, 2):
            remote(o_x(e), o_x(e), ox_send.at[e], ox_recv.at[e], at_x(e)).wait_recv()
        for by in (1, 3, 2):
            remote(o_y(0, c), o_y(0, c), oy_send.at[by], oy_recv.at[by], at_y(by)).start()
        remote(o_y(0, c), o_y(0, c), os_send.at[0], os_recv.at[0], sib).start()

    def out_side():
        for by in (1, 3, 2):
            ref = o_y(by, c)
            remote(ref, ref, oy_send.at[by], oy_recv.at[by], at_y(by)).wait_recv()
            remote(ref, ref, os_send.at[by], os_recv.at[by], sib).start()

    def out_end():
        for by in range(NY):
            ref = o_y(by, 1 - c)
            remote(ref, ref, os_send.at[by], os_recv.at[by], sib).wait_recv()

    out_across()

    lw_up, lw_down, lw_far = (wrap(y + k, NY) * 2 + c for k in (1, -1, 2))

    def lw_half(slot, d):
        return lwg.at[slot, pl.ds(d * (D // 2), D // 2)]

    def hop(ref, k, device=sib):
        return remote(ref, ref, l_send.at[k], l_recv.at[k], device)

    def side(ref, k):
        return remote(ref, ref, ls_send.at[k], ls_recv.at[k], sib)

    hop(lwg.at[r], 0, at_y(1)).start()
    hop(lwg.at[r], 1, at_y(-1)).start()
    side(lwg.at[r], 0).start()

    def lw_step_two():
        hop(lwg.at[lw_down], 0).wait_recv()
        hop(lwg.at[lw_up], 1).wait_recv()
        hop(lw_half(lw_down, 0), 2, at_y(1)).start()
        hop(lw_half(lw_up, 1), 3, at_y(-1)).start()
        side(lwg.at[lw_down], 1).start()
        side(lwg.at[lw_up], 2).start()

    def lw_step_three():
        hop(lw_half(lw_far, 0), 2).wait_recv()
        hop(lw_half(lw_far, 1), 3).wait_recv()
        side(lwg.at[lw_far], 3).start()

    def round_two(v):
        if v == 1:
            for e in (1, 3, 2):
                across_wait(m_across(1, e), xm_recv, e)
            ring_start(1, m_ring(v), zm_send, zm_recv)
        else:
            memory_next(v, 1)
        ring_next(v, 2)

    def round_three(v):
        if v == 1:
            memory_next(v, 1)
            ring_next(v, 3)
        else:
            ring_next(v, 3)
            memory_next(v, 2)

    def round_four(v):
        if v == 1:
            memory_next(v, 2)
            ring_next(v, 4)
        else:
            ring_next(v, 4)
            memory_next(v, 3)

    def round_five(v):
        memory_next(v, 3 if v == 1 else 4)

    def round_six(v):
        if v == 1:
            memory_next(v, 4)
        else:
            for e in (1, 3, 2):
                across_wait(m_across(0, e), xm_recv, e)

    def x_next(e):
        def one(v):
            across_wait(w_across(v, e), xw_recv, e)
            to_sibling(v, e).start()

        per_core(one)

    def far_piece(rec):
        return wg.at[:, group(2), :, :, :, pl.ds(pl.multiple_of(rec * 128, 128), 128)]

    def far_z(o):
        return wg.at[:, group(2), o, :, :, lanes]

    def far_along():
        remote(far_z(z), far_z(z), x2_send.at[0], x2_recv.at[0], at_x(2)).wait_recv()
        for d in (4, 3, 5, 2, 6, 1, 7):
            remote(far_z(z), far_z(z), z2_send.at[d], z2_recv.at[d], at_z(d)).start()

    def far_up():
        for d in range(1, NZ):
            ref = far_z(wrap(z - d, NZ))
            remote(ref, ref, z2_send.at[d], z2_recv.at[d], at_z(d)).wait_recv()
        ref = far_piece(r)
        for by in (1, 3, 2):
            remote(ref, ref, y2_send.at[by], y2_recv.at[by], at_y(by)).start()
        remote(ref, ref, s2_send.at[0], s2_recv.at[0], sib).start()

    def far_side():
        for by in (1, 3, 2):
            ref = far_piece(wrap(y - by, NY) * 2 + c)
            remote(ref, ref, y2_send.at[by], y2_recv.at[by], at_y(by)).wait_recv()
            remote(ref, ref, s2_send.at[by], s2_recv.at[by], sib).start()

    def far_end():
        for by in range(NY):
            ref = far_piece(wrap(y - by, NY) * 2 + 1 - c)
            remote(ref, ref, s2_send.at[by], s2_recv.at[by], sib).wait_recv()

    per_core(round_two)
    per_core(round_three)
    out_up()
    per_core(round_four)
    far_along()
    per_core(round_five)
    from_sibling(0)
    right.wait()
    lane_head = lax.broadcasted_iota(jnp.int32, (1, GW), 1) // HEAD

    def project_frames(g):
        a = xs[...]
        q = dot_nt(a, wg[0, g].reshape(GW, D))[:F] * (HEAD**-0.5 * LOG2E)
        for h in range(4):
            q4[:, h * QB : (h + 1) * QB, :] = (
                jnp.where(lane_head == h, q, 0.0).astype(BF).reshape(F // QB, QB, GW)
            )
        for n, ref in ((1, kk), (2, vv)):
            ref[pl.ds(MEM, F + 16), :] = dot_nt(a, wg[n, g].reshape(GW, D)).astype(BF)

    project_frames(x)
    per_core(round_six)

    def before_projection(j):
        @pl.when(j == 1)
        def _():
            from_sibling(1)

        @pl.when(j == 2)
        def _():
            from_sibling(3)

        @pl.when(j == 3)
        def _():
            far_end()

    def after_projection(j):
        @pl.when(j == 0)
        def _():
            x_next(1)
            far_up()

        @pl.when(j == 1)
        def _():
            out_side()

        @pl.when(j == 3)
        def _():
            lw_step_two()

    def after_attention(j):
        @pl.when(j == 0)
        def _():
            x_next(3)

        @pl.when(j == 2)
        def _():
            far_side()

    @pl.loop(0, G)
    def _(j):
        before_projection(j)
        g = wrap(x - (j + (j // 2) * (5 - 2 * j)), NX)

        @pl.when(j > 0)
        def _():
            project_frames(g)

        m = mg[...].reshape(MEM, D)
        for n, ref in ((1, kk), (2, vv)):
            ref[pl.ds(0, MEM), :] = dot_nt(m, wg[n, g].reshape(GW, D)).astype(BF)
        after_projection(j)
        columns = pl.ds(pl.multiple_of(g * GW, GW), GW)
        for b in range(F // QB):
            near = pl.ds(MEM + b * QB, 2 * QB)
            q = q4[b]
            s = jnp.concatenate([dot_nt(q, kk[pl.ds(0, MEM), :]), dot_nt(q, kk[near, :])], axis=1)
            s = (s.reshape(4, QB, KW) + bias[b][None]).reshape(4 * QB, KW)
            peak = jnp.max(s, axis=1, keepdims=True)
            w = jnp.exp2(s - peak)
            total = jnp.sum(w, axis=1, keepdims=True)
            w = w.astype(BF)
            o = dot_nn(w[:, :MEM], vv[pl.ds(0, MEM), :]) + dot_nn(w[:, MEM:], vv[near, :])
            o, total = o.reshape(4, QB, GW), total.reshape(4, QB, 1)
            out, den = o[3], jnp.broadcast_to(total[3], (QB, GW))
            for h in range(3):
                out = jnp.where(lane_head == h, o[h], out)
                den = jnp.where(lane_head == h, total[h], den)
            att[b * QB : (b + 1) * QB, columns] = (out / den).astype(BF)
        after_attention(j)

    out_end()

    for ch in range(NCH):
        features = slice(ch * CH, (ch + 1) * CH)
        w = owg[pl.ds(ch * (NX // NCH), NX // NCH)].reshape(CH, D)
        for b in range(2):
            rows = slice(b * 256, (b + 1) * 256)
            o = dot_nt(att[rows, :], w)
            live = first_frame + b * 256 + lax.broadcasted_iota(jnp.int32, (256, 1), 0) < length
            enc[rows, features] = jnp.where(
                live, frames[rows, features].astype(F32) + o, 0.0
            ).astype(BF)
        sent = dot_nn(ri[...], enc[:, features]) / cnt[:, :1]
        sb[ch] = sent.reshape(N_TM, CAP, CH).astype(BF)

        @pl.loop(1, N_TM)
        def _(d):
            to = lax.rem(t + d, N_TM)
            remote(sb.at[ch, to], rb.at[ch, t], a_send.at[ch, d], a_recv.at[ch, d], (r, to)).start()

        rb[ch, t] = sb[ch, t]

    enc_out = pltpu.make_async_copy(enc, enc_hbm, out_sem.at[0])
    enc_out.start()
    lw_step_three()

    def sent_core(v):
        for e in (1, 2, 3):
            if e != 2:
                ref = w_group(v, 0)
                remote(ref, ref, xw_send.at[e], xw_recv.at[e], sib).wait_send()
            ref = mg.at[x] if v == 0 else mg.at[x, z]
            remote(ref, ref, xm_send.at[e], xm_recv.at[e], sib).wait_send()
        for e in (0, 1, 3):
            to_sibling(v, e).wait_send()

    per_core(sent_core)
    remote(far_z(z), far_z(z), x2_send.at[0], x2_recv.at[0], sib).wait_send()
    for d in range(1, NZ):
        remote(far_z(z), far_z(z), z2_send.at[d], z2_recv.at[d], sib).wait_send()
    for by in range(NY):
        ref = far_piece(wrap(y - by, NY) * 2 + c)
        remote(ref, ref, s2_send.at[by], s2_recv.at[by], sib).wait_send()
        if by:
            remote(ref, ref, y2_send.at[by], y2_recv.at[by], sib).wait_send()
    for d in range(1, NZ):
        remote(o_z(z), o_z(z), oz_send.at[d], oz_recv.at[d], sib).wait_send()
    for e in (1, 2, 3):
        remote(o_x(0), o_x(0), ox_send.at[e], ox_recv.at[e], sib).wait_send()
        remote(o_y(0, c), o_y(0, c), oy_send.at[e], oy_recv.at[e], sib).wait_send()
    for by in range(NY):
        ref = o_y(by, c)
        remote(ref, ref, os_send.at[by], os_recv.at[by], sib).wait_send()
    for k, slot in enumerate((r, lw_down, lw_up, lw_far)):
        side(lwg.at[slot], k).wait_send()
        side(lwg.at[slot + 1 - 2 * c], k).wait_recv()
    hop(lwg.at[r], 0).wait_send()
    hop(lwg.at[r], 1).wait_send()
    hop(lw_half(r, 0), 2).wait_send()
    hop(lw_half(r, 0), 3).wait_send()

    def lm_out(k):
        return pltpu.make_async_copy(
            lmo.at[k], lm_hbm.at[:, pl.ds(k * 256, 256)], out_sem.at[1 + k]
        )

    for ch in range(NCH):

        @pl.loop(1, N_TM)
        def _(d):
            to = lax.rem(t + d, N_TM)
            source = wrap(t - d, N_TM)
            copy = remote(
                sb.at[ch, to], rb.at[ch, source], a_send.at[ch, d], a_recv.at[ch, d], (r, to)
            )
            copy.wait_recv()
            copy.wait_send()

        got = rb[ch].astype(F32).reshape(SLOTS, CH).astype(BF)
        for k in range(2 * NY):
            part = dot_nn(got, lwg[k, ch * CH : (ch + 1) * CH, :])
            if ch > 0:
                part += lacc[k]
            if ch < NCH - 1:
                lacc[k] = part
            else:
                lmo[k] = part.astype(BF)
                lm_out(k).start()
    enc_out.wait()
    for k in range(2 * NY):
        lm_out(k).wait()


def per_device(
    frames, lengths, norm_gain, memory_gain, qkv_weight, out_weight, segment_ids, owners, language_weight
):
    vmem = pl.BlockSpec(memory_space=pltpu.VMEM)
    smem = pl.BlockSpec(memory_space=pltpu.SMEM)
    hbm = pl.BlockSpec(memory_space=pl.ANY)
    dma = pltpu.SemaphoreType.DMA
    enc, lm = pl.pallas_call(
        kernel,
        out_shape=(
            jax.ShapeDtypeStruct((F, D), BF),
            jax.ShapeDtypeStruct((SLOTS, DL), BF),
        ),
        in_specs=[vmem, smem, vmem, vmem, hbm, hbm, vmem, vmem, hbm],
        out_specs=(hbm, hbm),
        scratch_shapes=[
            pltpu.VMEM((3, NX, NZ, 2, 16, D), BF),
            pltpu.VMEM((NX, NZ, 32, D), BF),
            pltpu.VMEM((2 * NY, D, DL // (2 * NY)), BF),
            pltpu.VMEM((F + 16, D), BF),
            pltpu.VMEM((NX, NZ, 16, D), BF),
            pltpu.VMEM((F // C, D), F32),
            pltpu.VMEM((F // QB, 4 * QB, GW), BF),
            pltpu.VMEM((MEM + F + QB, GW), BF),
            pltpu.VMEM((MEM + F + QB, GW), BF),
            pltpu.VMEM((F, D), BF),
            pltpu.VMEM((F // QB, QB, KW), F32),
            pltpu.VMEM((SLOTS, F), BF),
            pltpu.VMEM((SLOTS, 128), F32),
            pltpu.VMEM((F, D), BF),
            pltpu.VMEM((NCH, N_TM, CAP, CH), BF),
            pltpu.VMEM((NCH, N_TM, CAP, CH), BF),
            pltpu.VMEM((2 * NY, SLOTS, 256), F32),
            pltpu.VMEM((2 * NY, SLOTS, DL // (2 * NY)), BF),
            dma((8,)), dma((8,)), dma((8,)), dma((8,)), dma((4,)), dma((4,)), dma((4,)), dma((4,)),
            dma((4,)), dma((4,)),
            dma((1,)), dma((1,)), dma((8,)), dma((8,)), dma((4,)), dma((4,)), dma((4,)), dma((4,)),
            dma((8,)), dma((8,)), dma((4,)), dma((4,)), dma((4,)), dma((4,)), dma((4,)), dma((4,)),
            dma((1,)), dma((1,)), dma((4,)), dma((4,)), dma((4,)), dma((4,)),
            dma((NCH, N_TM)), dma((NCH, N_TM)), dma((3,)), dma((1 + 2 * NY,)),
        ],
        compiler_params=pltpu.CompilerParams(
            collective_id=0, has_side_effects=True, vmem_limit_bytes=58 * 2**20
        ),
        name="block",
    )(
        frames[0],
        lengths,
        norm_gain[None],
        memory_gain[None],
        qkv_weight.transpose(0, 2, 1).reshape(3, 2, 16, D),
        out_weight.T,
        segment_ids[0],
        owners[0, :, :, 0],
        language_weight,
    )
    return (enc[None], lm[None, None])


def solution(mesh):
    in_specs = (
        P("rec", "tm", None),
        P("rec"),
        P(),
        P(),
        P(None, None, "tm"),
        P(None, "tm"),
        P("rec", "tm", None),
        P("rec", "tm", None, None),
        P(None, "rec"),
    )
    out_specs = (P("rec", "tm", None), P("rec", "tm", None, None))
    return jax.shard_map(
        per_device, mesh=mesh, in_specs=in_specs, out_specs=out_specs, check_vma=False
    )
```
